32 devices in a mesh: groups: 2 (over y), seq: 4 (over z), head: 2 (over x), dp: 2 (over core).
Axes of the slice: x: 2, y: 2, z: 4, core: 2. Of those that a mesh axis runs over, the one named last changes fastest.
Arguments:
- inputs: bfloat16 [4, 2048, 3072], P(('groups', 'dp'), 'seq'), parts along dimension 0, may hold values from -6 to 6
- queries: bfloat16 [4, 2048, 4096], P(('groups', 'dp'), 'seq', 'head'), parts along dimension 0, may hold values from -6 to 6
- keys: bfloat16 [4, 2048, 4096], P(('groups', 'dp'), 'seq', 'head'), parts along dimension 0, may hold values from -6 to 6
- values: bfloat16 [4, 2048, 4096], P(('groups', 'dp'), 'seq', 'head'), parts along dimension 0, may hold values from -6 to 6
- log_decay: float32 [4, 32, 2048], P(('groups', 'dp'), 'head', 'seq'), parts along dimension 0, may hold values from -0.85 to 0, as said below
- list_lengths: int32 [4, 4], P(('groups', 'dp')), parts along dimension 0, may hold values from 1 to 1024, 2048 in all within a row
- grad_out: bfloat16 [4, 2048, 4096], P(('groups', 'dp'), 'seq', 'head'), parts along dimension 0, may hold values from -6 to 6
Outputs:
- grad_queries: bfloat16 [4, 2048, 4096], P(('groups', 'dp'), 'seq', 'head'), parts along dimension 0
- grad_values: bfloat16 [4, 2048, 4096], P(('groups', 'dp'), 'seq', 'head'), parts along dimension 0
- grad_w_key: float32 [6144, 4096], P(('groups', 'seq', 'dp'), 'head'), parts along dimension 0
The draws below stay inside these ranges and needn't reach their ends.
There are 2 independent parts, one for each index of `groups`. The reference program is written for one: setup_inputs(seed, part) draws one part's arguments, and reference() takes and returns one part's arrays. A program takes and returns all parts, laid end to end along the dimension named above; each array names one. Nothing has to cross between parts.
Inputs may be any that keep to these rules, and one draw needn't show every extreme that they name: `list_lengths`: each row's 4 list lengths sum to 2048. `log_decay`: negative at every position and head.
All inputs are finite; a program needn't handle non-finite values.
Results may differ from the reference program's by a relative error of at most 0.02.
Values may be sent and summed in bfloat16 or wider, within the bound.
A program may use at most 192 MiB of HBM per device.

```python
import math
import jax
import jax.numpy as jnp
import numpy as np
from jax import lax

D = 3072
H = 32
HD = 128
BLOCK = 512
NLIST = 4
SEQS = 2
SEQ_LEN = 2048
N_DP = 2


def draw_log_decay(key, part):
    streams = jax.random.split(jax.random.fold_in(key, 11), 7)
    slow_share = 0.5
    slow = jax.random.uniform(streams[0], (SEQS, H, 1)) < slow_share
    slow_rate = jnp.exp(jax.random.uniform(streams[1], (SEQS, H, 1), minval=math.log(0.1), maxval=math.log(0.5))) / SEQ_LEN
    fast_rate = jax.random.uniform(streams[2], (SEQS, H, 1), minval=2.3 / 50.0, maxval=2.3 / 30.0)
    forgetting_rate = jnp.where(slow, slow_rate, fast_rate)
    pieces = SEQ_LEN // BLOCK
    replica_factor = jax.random.uniform(streams[3], (SEQS, H, pieces, 1), minval=0.35, maxval=1.0)
    replica_factor = jnp.broadcast_to(replica_factor, (SEQS, H, pieces, BLOCK)).reshape(SEQS, H, SEQ_LEN)
    rough_estimate = jax.random.uniform(streams[4], (SEQS, H, SEQ_LEN), minval=0.5, maxval=1.5)
    third = SEQ_LEN // 3
    restart_indices = jnp.arange(3, dtype=jnp.int32)[None, :] * third + jax.random.randint(streams[5], (SEQS, 3), 0, third)
    stack_level = jnp.log(jax.random.uniform(streams[6], (SEQS, 3), minval=0.5, maxval=0.8))
    element_offsets = jnp.arange(SEQ_LEN, dtype=jnp.int32)
    contiguous_span_size = jnp.sum(jnp.where(element_offsets[None, None, :] == restart_indices[:, :, None], stack_level[:, :, None], 0.0), axis=1)
    return (-forgetting_rate * replica_factor * rough_estimate + contiguous_span_size[:, None, :]).astype(jnp.float32)


def strengthened(drawn, own_key, source, target, blocks, factor):
    owner, partner = [(jnp.arange(drawn.shape[position]) // (drawn.shape[position] // blocks)).reshape([-1 if axis == position else 1 for axis in range(drawn.ndim)]) for position in (source, target)]
    chosen = jax.random.permutation(own_key, blocks)[partner]
    strong = (owner == chosen) | (owner == (partner + blocks // 2) % blocks)
    return jnp.where(strong, factor * drawn, drawn)


def block_scale(own_key, dims, shards, least, top_value):
    loudness, own = 1.0, jax.random.fold_in(own_key, 6)
    for position, parts in shards:
        draws = jnp.exp(jax.random.uniform(jax.random.fold_in(own, position), (parts,), jnp.float32, least / len(shards), top_value / len(shards)))
        loudness = loudness * jnp.repeat(draws, dims[position] // parts).reshape([-1 if axis == position else 1 for axis in range(len(dims))])
    return loudness


def profile(number_of, total, bound, skew):
    weights = [(1 << 20) // math.isqrt(rank ** skew) + 1 for rank in range(2, number_of + 1)]
    spare, given = total - bound - (number_of - 1), [1] * (number_of - 1)
    while spare > 0:
        candidates = [i for i in range(number_of - 1) if given[i] < bound]
        mass, left = sum([weights[i] for i in candidates]), spare
        for i in candidates:
            addition = min(bound - given[i], max(1, left * weights[i] // mass), spare)
            given[i] = given[i] + addition
            spare = spare - addition
    return np.array([bound] + given)


def ragged_sizes(stream_key, number_of, total, bound, slope):
    if number_of == 2:
        one = jax.random.randint(stream_key, (), max(1, total - bound), min(bound, total - 1) + 1)
        return jnp.stack([one, total - one])
    sizes = jnp.asarray(profile(number_of, total, bound, slope), jnp.int32)
    pairs = (number_of - 1) // 2
    source_of, sink = sizes[1:1 + 2 * pairs:2], sizes[2:2 + 2 * pairs:2]
    room = jnp.minimum(source_of - 1, bound - sink)
    moved = jax.random.randint(jax.random.fold_in(stream_key, 1), (pairs,), 0, 1 << 20) % (room + 1)
    sizes = sizes.at[1:1 + 2 * pairs:2].set(source_of - moved).at[2:2 + 2 * pairs:2].set(sink + moved)
    return sizes[jax.random.permutation(jax.random.fold_in(stream_key, 2), number_of)]


def noise(rng, dims, deviation, limit, cuts=(), held_as=jnp.bfloat16):
    values = jax.random.normal(rng, dims, jnp.float32) * deviation
    if len(cuts) > 0:
        values = block_scale(rng, dims, cuts, -0.22, 0.18) * values
    return jnp.clip(values, min=-limit, max=limit).astype(held_as)


def gaussian_with(stream_key, dims, spread, bound, cuts, heavy, held_as=jnp.bfloat16):
    drawn = spread * jax.random.normal(stream_key, dims, jnp.float32)
    if cuts:
        drawn = drawn * block_scale(stream_key, dims, cuts, -0.22, 0.18)
    return jnp.clip(strengthened(drawn, jax.random.fold_in(stream_key, 3), *heavy), -bound, bound).astype(held_as)


def setup_inputs(seed: int = 0, part: int = 0) -> dict:
    seeds = jax.random.split(jax.random.key(seed), 8)
    part_splits = jax.random.split(jax.random.fold_in(seeds[7], part), 8)
    inputs = gaussian_with(part_splits[0], (SEQS, SEQ_LEN, D), 1.0, 6.0, ((0, 2), (1, 4)), (1, 2, 4, 2.0))
    queries = noise(part_splits[1], (SEQS, SEQ_LEN, H * HD), 1.0, 6.0, ((0, 2), (1, 4), (2, 2)))
    keys = noise(part_splits[2], (SEQS, SEQ_LEN, H * HD), 1.0, 6.0, ((0, 2), (1, 4), (2, 2)))
    values = noise(part_splits[3], (SEQS, SEQ_LEN, H * HD), 1.0, 6.0, ((0, 2), (1, 4), (2, 2)))
    log_decay = draw_log_decay(jax.random.fold_in(jax.random.fold_in(seeds[7], part), 71), part)
    list_lengths = jax.vmap(lambda own: ragged_sizes(own, NLIST, SEQ_LEN, SEQ_LEN // 2, 0))(jax.random.split(part_splits[5], SEQS)).reshape((SEQS, NLIST)).astype(jnp.int32)
    grad_out = noise(part_splits[6], (SEQS, SEQ_LEN, H * HD), 1.0, 6.0, ((0, 2), (1, 4), (2, 2)))
    return dict(inputs=inputs, queries=queries, keys=keys, values=values, log_decay=log_decay, list_lengths=list_lengths, grad_out=grad_out)


EPS = 1e-06

def segment_ids(list_lengths, first, count):
    starts = jnp.cumsum(list_lengths, axis=-1) - list_lengths
    element_offsets = first + jnp.arange(count, dtype=jnp.int32)
    segment = lax.optimization_barrier(jnp.sum((starts[:, None, :] <= element_offsets[None, :, None]).astype(jnp.int32), axis=-1))
    before = lax.optimization_barrier(jnp.sum((starts <= first - 1).astype(jnp.int32), axis=-1))
    return (segment, before)

def gate_tables(log_dec, segment, before):
    cumulative = jnp.cumsum(log_dec, axis=-1)
    last = cumulative[..., -1:]
    seg_end = segment[:, -1:]
    open_in = (segment == before[:, None])[:, None, :]
    open_out = (segment == seg_end)[:, None, :]
    gamma = jnp.where(open_in, jnp.exp(cumulative), 0.0)
    weight = jnp.where(open_out, jnp.exp(last - cumulative), 0.0)
    passing = jnp.where((seg_end[:, 0] == before)[:, None], jnp.exp(last[..., 0]), 0.0)
    return (cumulative, gamma, weight, passing)

def decay_matrix(cumulative, segment):
    count = segment.shape[-1]
    order = jnp.arange(count, dtype=jnp.int32)
    same = (segment[:, :, None] == segment[:, None, :]) & (order[:, None] >= order[None, :])
    same = same[:, None]
    gap = jnp.where(same, cumulative[..., :, None] - cumulative[..., None, :], 0.0)
    return jnp.where(same, jnp.exp(gap), 0.0)

def product32(form, left, right):
    return jnp.einsum(form, left.astype(jnp.float32), right.astype(jnp.float32))

def reference(inputs, queries, keys, values, log_decay, list_lengths, grad_out):
    seq_count, length, width = inputs.shape
    heads = log_decay.shape[1]
    head_dim = queries.shape[-1] // heads
    blocks = length // BLOCK

    def split(array):
        return array.reshape(seq_count, blocks, BLOCK, heads, head_dim).transpose(1, 0, 2, 3, 4)
    query_all = split(queries)
    key_all = split(keys)
    value_all = split(values)
    grad_all = split(grad_out)
    decay_all = log_decay.reshape(seq_count, heads, blocks, BLOCK).transpose(2, 0, 1, 3)
    rows_all = inputs.reshape(seq_count, blocks, BLOCK, width).transpose(1, 0, 2, 3)
    firsts = jnp.arange(blocks, dtype=jnp.int32) * BLOCK

    def summary(item):
        key_blk, value_blk, decay_blk, first = item
        segment, before = segment_ids(list_lengths, first, BLOCK)
        cumulative, gamma, weight, passing = gate_tables(decay_blk, segment, before)
        weight_rows = jnp.transpose(weight, (0, 2, 1))[..., None]
        weighted_keys = (key_blk.astype(jnp.float32) * weight_rows).astype(jnp.bfloat16)
        return (passing, product32('suhe,suhf->shef', weighted_keys, value_blk))
    passings, updates = lax.map(summary, (key_all, value_all, decay_all, firsts))

    def forward_step(state, item):
        passing, update = item
        return (passing[..., None, None] * state + update, state)
    _, states_in = lax.scan(forward_step, jnp.zeros(updates.shape[1:], jnp.float32), (passings, updates))

    def main(item):
        query_blk, key_blk, value_blk, grad_blk, decay_blk, first, state = item
        segment, before = segment_ids(list_lengths, first, BLOCK)
        cumulative, gamma, weight, passing = gate_tables(decay_blk, segment, before)
        decay = decay_matrix(cumulative, segment)
        state_bf = state.astype(jnp.bfloat16)
        gamma_rows = jnp.transpose(gamma, (0, 2, 1))[..., None]
        scores_bf = (product32('sthe,suhe->shtu', query_blk, key_blk) * decay).astype(jnp.bfloat16)
        attended = gamma_rows * product32('sthe,shef->sthf', query_blk, state_bf) + product32('shtu,suhf->sthf', scores_bf, value_blk)
        inverse = lax.rsqrt(lax.optimization_barrier(jnp.mean(attended * attended, axis=-1, keepdims=True)) + EPS)
        normed = attended * inverse
        grad_wide = grad_blk.astype(jnp.float32)
        grad_attended = (inverse * (grad_wide - normed * lax.optimization_barrier(jnp.mean(grad_wide * normed, axis=-1, keepdims=True)))).astype(jnp.bfloat16)
        gated_queries = (query_blk.astype(jnp.float32) * gamma_rows).astype(jnp.bfloat16)
        back_state = product32('sthe,sthf->shef', gated_queries, grad_attended)
        grad_scores = (product32('sthf,suhf->shtu', grad_attended, value_blk) * decay).astype(jnp.bfloat16)
        grad_query = gamma_rows * product32('sthf,shef->sthe', grad_attended, state_bf) + product32('shtu,suhe->sthe', grad_scores, key_blk)
        key_inner = product32('shtu,sthe->suhe', grad_scores, query_blk)
        value_inner = product32('shtu,sthf->suhf', scores_bf, grad_attended)
        return (grad_query.astype(jnp.bfloat16), key_inner, value_inner, back_state)
    grad_qs, key_inners, value_inners, back_states = lax.map(main, (query_all, key_all, value_all, grad_all, decay_all, firsts, states_in))

    def backward_step(later, item):
        passing, back_state = item
        return (back_state + passing[..., None, None] * later, later)
    _, laters = lax.scan(backward_step, jnp.zeros(back_states.shape[1:], jnp.float32), (passings, back_states), reverse=True)

    def finish(total, item):
        key_blk, value_blk, rows_blk, key_inner, value_inner, decay_blk, first, later = item
        segment, before = segment_ids(list_lengths, first, BLOCK)
        cumulative, gamma, weight, passing = gate_tables(decay_blk, segment, before)
        weight_rows = jnp.transpose(weight, (0, 2, 1))[..., None]
        later_bf = later.astype(jnp.bfloat16)
        grad_key = (key_inner + weight_rows * product32('suhf,shef->suhe', value_blk, later_bf)).astype(jnp.bfloat16)
        grad_value = (value_inner + weight_rows * product32('suhe,shef->suhf', key_blk, later_bf)).astype(jnp.bfloat16)
        grouped_rows = rows_blk.reshape(N_DP, seq_count // N_DP, BLOCK, width)
        grouped_keys = grad_key.reshape(N_DP, seq_count // N_DP, BLOCK, heads * head_dim)
        partial_value = product32('psud,psuf->pdf', grouped_rows, grouped_keys)
        partial_value = lax.optimization_barrier(partial_value.astype(jnp.bfloat16))
        return (total + lax.optimization_barrier(jnp.sum(partial_value.astype(jnp.float32), axis=0)), grad_value)
    grad_w_key, grad_vs = lax.scan(finish, jnp.zeros((width, heads * head_dim), jnp.float32), (key_all, value_all, rows_all, key_inners, value_inners, decay_all, firsts, laters))

    def join(array):
        return array.transpose(1, 0, 2, 3, 4).reshape(seq_count, length, heads * head_dim)
    return (join(grad_qs), join(grad_vs), grad_w_key)
```

```python
import functools
import math

import jax
import jax.numpy as jnp
from jax import lax
from jax.experimental import pallas as pl
from jax.experimental.pallas import tpu as pltpu
from jax.sharding import PartitionSpec as P

EPS = 1e-06
MESH = pl.DeviceIdType.MESH
LANES = 128
F32 = jnp.float32
BF16 = jnp.bfloat16


def dot(a, b, ca, cb):
    return lax.dot_general(a, b, (((ca,), (cb,)), ((), ())), preferred_element_type=F32)


def greet(pair):
    barrier = pltpu.get_barrier_semaphore()
    me = lax.axis_index("seq")
    n = lax.axis_size("seq")

    @pl.when(me > 0)
    def _():
        pl.semaphore_signal(barrier, inc=1, device_id={"seq": me - 1}, device_id_type=MESH)

    @pl.when(me < n - 1)
    def _():
        pl.semaphore_signal(barrier, inc=1, device_id={"seq": me + 1}, device_id_type=MESH)

    peers = (me > 0).astype(jnp.int32) + (me < n - 1).astype(jnp.int32) + 1
    mate = 1 - lax.axis_index("dp")
    pl.semaphore_signal(barrier, inc=1, device_id={"dp": mate}, device_id_type=MESH)
    if pair is not None:
        pl.semaphore_signal(barrier, inc=1, device_id={"head": pair}, device_id_type=MESH)
        peers = peers + 1
    return lambda: pl.semaphore_wait(barrier, peers)


def sizes(heads, D):
    group = math.gcd(heads, 2)
    n = lax.axis_size("seq")
    return n, group, heads // group, D // (2 * n)


def repeat(count, body):
    if count <= 3:
        for i in range(count):
            body(i)
        return

    def step(i, c):
        body(i)
        return c

    lax.fori_loop(0, count, step, 0)


LAG = 6


def layer_kernel(
    heads, ll_ref, ld_ref, x_hbm, q_hbm, k_hbm, v_hbm, g_hbm, gq_hbm, gv_hbm, gw_hbm,
    q_ref, k_ref, v_ref, g_ref, x_ref, xt_ref, xm_ref, xe_ref, gm_ref, ge_ref, st_ref, out_ref,
    cum_ref, colb_ref, mask_ref, min_ref, mout_ref, upd_ref, att_ref, sc_ref, ga_ref,
    bs_ref, ki_ref, vi_ref, fsend, frecv, bsend, brecv, fss, frs, bss, brs,
    load_sem, x_sem, store_sem, xss, xrs, gss, grs, ss, rs, ess, ers, pss, prs, hss, hrs, mss, mrs,
):
    me = lax.axis_index("seq")
    dp = lax.axis_index("dp")
    hx = lax.axis_index("head")
    B, D = x_ref.shape
    n, group, groups, rows = sizes(heads, D)
    first = me * B
    mate = 1 - dp
    width = group * LANES
    paired = lax.axis_size("head") % 2 == 0
    half = rows // 2 if paired else rows
    side = hx % 2 if paired else 0
    pair = hx + 1 - 2 * side if paired else None
    late = n - 2
    lead = (late + 1) // 2

    is_end = (me == 0) | (me == n - 1)
    is_hub = (me == 1) | (me == n - 2)
    inside = jnp.logical_not(is_end)
    low = me <= 1
    hub = jnp.where(low, 1, n - 2)
    ext = jnp.where(low, 0, n - 1)

    def far(e):
        return jnp.where(low, n - 1 - e, e)

    def columns(g):
        return pl.ds(pl.multiple_of(g * width, LANES), width)

    def load(a, g):
        src = (k_hbm, v_hbm, q_hbm, g_hbm)[a]
        dst = (k_ref, v_ref, q_ref, g_ref)[a]
        return pltpu.make_async_copy(
            src.at[:, columns(g)], dst.at[:, columns(g)], load_sem.at[a, g]
        )

    def store(a, g):
        src, dst = ((q_ref, gq_hbm), (g_ref, gv_hbm), (out_ref, gw_hbm))[a]
        return pltpu.make_async_copy(
            src.at[:, columns(g)], dst.at[:, columns(g)], store_sem.at[a, g]
        )

    def each_group(body, start=0):
        def step(g, c):
            body(g)
            return c
        lax.fori_loop(start, groups, step, 0)

    greeted = greet(pair)

    load(0, 0).start()
    load(1, 0).start()
    load_x = pltpu.make_async_copy(x_hbm, x_ref, x_sem)
    load_x.start()
    load(0, 1).start()
    load(1, 1).start()
    for a in (2, 3):
        for g in (0, 1):
            load(a, g).start()

    def load_rest(g):
        for a in range(4):
            load(a, g).start()

    each_group(load_rest, 2)

    lengths = [ll_ref[0, i] for i in range(ll_ref.shape[1])]
    starts = [jnp.int32(0)]
    for length in lengths[:-1]:
        starts.append(starts[-1] + length)

    def seg_of(pos):
        total = (starts[0] <= pos).astype(jnp.int32)
        for s in starts[1:]:
            total = total + (s <= pos).astype(jnp.int32)
        return total

    before = seg_of(first - 1)
    end = seg_of(first + B - 1)
    seg_col = seg_of(first + lax.broadcasted_iota(jnp.int32, (B, LANES), 0))
    min_ref[...] = jnp.where(seg_col == before, 1.0, 0.0).astype(F32)
    mout_ref[...] = jnp.where(seg_col == end, 1.0, 0.0).astype(F32)
    open_all = jnp.where(jnp.full((1, LANES), end) == before, 1.0, 0.0).astype(F32)
    t_pos = lax.broadcasted_iota(jnp.int32, (B, B), 0)
    u_pos = lax.broadcasted_iota(jnp.int32, (B, B), 1)
    tri = jnp.where(t_pos <= u_pos, 1.0, 0.0).astype(F32)
    cum_ref[...] = lax.dot_general(
        ld_ref[...], tri, (((1,), (0,)), ((), ())),
        preferred_element_type=F32, precision=lax.Precision.HIGHEST,
    )

    def make_mask():
        wide = jnp.concatenate([seg_col] * (B // LANES), axis=1)
        row = seg_of(first + lax.broadcasted_iota(jnp.int32, (1, B), 1))
        same = (t_pos >= u_pos) & (wide == row)
        mask_ref[...] = jnp.where(same, 0.0, -1e30).astype(F32)

    def lanes(h):
        return pl.ds(pl.multiple_of(h * LANES, LANES), LANES)

    def weight_of(h):
        cb = colb_ref[h]
        return jnp.exp(cb[B - 1 : B, :] - cb) * mout_ref[...]

    def gamma_of(h):
        return jnp.exp(colb_ref[h]) * min_ref[...]

    def passing_of(h):
        return jnp.exp(colb_ref[h, B - 1 : B, :]) * open_all

    def decay_of(h, ts, cols):
        cb = colb_ref[h, ts, :]
        wide = jnp.concatenate([cb] * (cols // LANES), axis=1)
        row = cum_ref[pl.ds(h, 1), :cols]
        return jnp.exp((wide - row) + mask_ref[ts, :cols])

    def each_head(g, body):
        for i in range(group):
            body(g * group + i, i)

    def hop(src, dst, ss, rs, g, to):
        span = pl.ds(g * group, group)
        return pltpu.make_async_remote_copy(
            src_ref=src.at[span], dst_ref=dst.at[span], send_sem=ss.at[g], recv_sem=rs.at[g],
            device_id={"seq": to}, device_id_type=MESH,
        )

    def forward(g):
        return hop(fsend, frecv, fss, frs, g, me + 1)

    def backward(g):
        return hop(bsend, brecv, bss, brs, g, me - 1)

    def update(g):
        load(0, g).wait()
        load(1, g).wait()

        def one(h, i):
            colb_ref[h] = jnp.transpose(jnp.broadcast_to(cum_ref[pl.ds(h, 1), :], (LANES, B)))
            wk = (k_ref[:, lanes(h)].astype(F32) * weight_of(h)).astype(BF16)
            upd_ref[h] = dot(wk, v_ref[:, lanes(h)], 0, 0)

        each_head(g, one)

        @pl.when(me == 0)
        def _():
            def ready(h, i):
                fsend[h] = upd_ref[h].astype(BF16)
                frecv[h] = jnp.zeros((LANES, LANES), BF16)
            each_head(g, ready)
            forward(g).start()

        @pl.when(me == n - 1)
        def _():
            def ready(h, i):
                brecv[h] = jnp.zeros((LANES, LANES), BF16)
            each_head(g, ready)

    def relay_forward(g):
        @pl.when(inside)
        def _():
            forward(g).wait_recv()

            def send(h, i):
                fsend[h] = (passing_of(h) * frecv[h].astype(F32) + upd_ref[h]).astype(BF16)
            each_head(g, send)
            forward(g).start()

    def scores(g):
        load(2, g).wait()

        def one(h, i):
            s = dot(q_ref[:, lanes(h)], k_ref[:, lanes(h)], 1, 1)
            s_bf = (s * decay_of(h, slice(0, B), B)).astype(BF16)
            sc_ref[i] = s_bf
            att_ref[i] = dot(s_bf, v_ref[:, lanes(h)], 1, 0)

        each_head(g, one)

    def attend(g):
        load(3, g).wait()

        @pl.when(me == n - 1)
        def _():
            forward(g).wait_recv()

        def one(h, i):
            gamma = gamma_of(h)
            q = q_ref[:, lanes(h)]
            att = gamma * dot(q, frecv[h], 1, 0) + att_ref[i]
            inv = lax.rsqrt(jnp.mean(att * att, axis=-1, keepdims=True) + EPS)
            normed = att * inv
            wide = g_ref[:, lanes(h)].astype(F32)
            ga = (inv * (wide - normed * jnp.mean(wide * normed, axis=-1, keepdims=True))).astype(BF16)
            ga_ref[i] = ga
            gated = (q.astype(F32) * gamma).astype(BF16)
            bs_ref[h] = dot(gated, ga, 0, 0)

        each_head(g, one)

        @pl.when(me == n - 1)
        def _():
            def ready(h, i):
                bsend[h] = bs_ref[h].astype(BF16)
            each_head(g, ready)
            backward(g).start()

    def relay_back(g):
        @pl.when(me < n - 1)
        def _():
            backward(g).wait_recv()

        @pl.when(inside)
        def _():
            def send(h, i):
                bsend[h] = (passing_of(h) * brecv[h].astype(F32) + bs_ref[h]).astype(BF16)
            each_head(g, send)
            backward(g).start()

    tile = math.gcd(B, 256)
    tiles = B // tile

    def grads(g):
        slot = (g % 2) * group

        def one(h, i):
            gamma = gamma_of(h)
            kis, vis = [None] * tiles, [None] * tiles
            for b in range(tiles):
                ts, cols = slice(b * tile, (b + 1) * tile), (b + 1) * tile
                ga = ga_ref[i, ts, :]
                q = q_ref[ts, lanes(h)]
                gs = (dot(ga, v_ref[:cols, lanes(h)], 1, 1) * decay_of(h, ts, cols)).astype(BF16)
                gq = gamma[ts] * dot(ga, frecv[h], 1, 1) + dot(gs, k_ref[:cols, lanes(h)], 1, 0)
                ki = dot(gs, q, 0, 0)
                vi = dot(sc_ref[i, ts, :cols], ga, 0, 0)
                q_ref[ts, lanes(h)] = gq.astype(BF16)
                for j in range(b + 1):
                    js = slice(j * tile, (j + 1) * tile)
                    kis[j] = ki[js] if kis[j] is None else kis[j] + ki[js]
                    vis[j] = vi[js] if vis[j] is None else vis[j] + vi[js]
            for j in range(tiles):
                ki_ref[slot + i, j * tile : (j + 1) * tile, :] = kis[j]
                vi_ref[slot + i, j * tile : (j + 1) * tile, :] = vis[j]

        each_head(g, one)
        store(0, g).start()

    def gk_copy(g):
        return pltpu.make_async_remote_copy(
            src_ref=k_ref.at[:, columns(g)], dst_ref=gm_ref.at[:, columns(g)],
            send_sem=gss.at[g], recv_sem=grs.at[g],
            device_id={"dp": mate}, device_id_type=MESH,
        )

    def ends_copy(g):
        return pltpu.make_async_remote_copy(
            src_ref=k_ref.at[:, columns(g)], dst_ref=ge_ref.at[pl.ds(0, B), columns(g)],
            send_sem=hss.at[g], recv_sem=hrs.at[g],
            device_id={"seq": hub}, device_id_type=MESH,
        )

    def pass_copy(g):
        return pltpu.make_async_remote_copy(
            src_ref=ge_ref.at[pl.ds(0, B), columns(g)], dst_ref=ge_ref.at[pl.ds(B, B), columns(g)],
            send_sem=mss.at[g], recv_sem=mrs.at[g],
            device_id={"dp": mate}, device_id_type=MESH,
        )

    def finish(g):
        slot = (g % 2) * group

        def one(h, i):
            w = weight_of(h)
            later = brecv[h]
            k = k_ref[:, lanes(h)]
            k_ref[:, lanes(h)] = (ki_ref[slot + i] + w * dot(v_ref[:, lanes(h)], later, 1, 1)).astype(BF16)
            g_ref[:, lanes(h)] = (vi_ref[slot + i] + w * dot(k, later, 1, 0)).astype(BF16)

        each_head(g, one)
        pl.when(is_end)(lambda: ends_copy(g).start())
        gk_copy(g).start()
        store(1, g).start()

    def share(z, owner):
        return pl.ds(pl.multiple_of((z * 2 + owner) * rows, math.gcd(rows, LANES)), rows)

    def halves(which, base=0):
        return pl.ds(pl.multiple_of(base + which * half, math.gcd(half, LANES)), half)

    def x_copy(z):
        return pltpu.make_async_remote_copy(
            src_ref=xt_ref.at[share(z, mate)], dst_ref=xm_ref.at[z],
            send_sem=xss.at[z], recv_sem=xrs.at[z],
            device_id={"dp": mate}, device_id_type=MESH,
        )

    def turn(i, c):
        span = pl.ds(pl.multiple_of(i * LANES, LANES), LANES)
        xt_ref[span, :] = jnp.transpose(x_ref[:, span])
        return c

    def turn_inputs():
        load_x.wait()
        if 2 * rows % LANES == 0:
            spans = 2 * rows // LANES

            def one(e):
                z = far(e)
                lax.fori_loop(z * spans, (z + 1) * spans, turn, 0)
                x_copy(z).start()
        else:
            lax.fori_loop(0, D // LANES, turn, 0)

            def one(e):
                x_copy(far(e)).start()

        lax.fori_loop(0, n, lambda e, c: (one(e), c)[1], 0)

    def early_copy(e, part):
        z = far(e)
        src = (
            xt_ref.at[halves(side, (z * 2 + dp) * rows)] if part == 0 else xm_ref.at[z, halves(side)]
        )
        return pltpu.make_async_remote_copy(
            src_ref=src, dst_ref=xe_ref.at[z, halves(side), pl.ds(part * B, B)],
            send_sem=ess.at[z, part], recv_sem=ers.at[z, part],
            device_id={"seq": hub}, device_id_type=MESH,
        )

    def pair_copy(e, part, which):
        z = far(e)
        ref = xe_ref.at[z, halves(which), pl.ds(part * B, B)]
        return pltpu.make_async_remote_copy(
            src_ref=ref, dst_ref=ref, send_sem=pss.at[z, part], recv_sem=prs.at[z, part],
            device_id={"head": pair}, device_id_type=MESH,
        )

    def send_early(lo, hi):
        def one(e):
            early_copy(lo + e, 0).start()
            x_copy(far(lo + e)).wait_recv()
            early_copy(lo + e, 1).start()
        pl.when(is_end)(lambda: repeat(hi - lo, one))

    def take_early(lo, hi):
        def one(e):
            for part in range(2):
                early_copy(lo + e, part).wait_recv()
                if paired:
                    pair_copy(lo + e, part, side).start()
        pl.when(is_hub)(lambda: repeat(hi - lo, one))

    def have_early(lo, count):
        if paired:
            def one(e):
                for part in range(2):
                    pair_copy(lo + e, part, 1 - side).wait_recv()
            repeat(count, one)

    def partial(z, g):
        own = dot(xt_ref[share(z, dp), :], k_ref[:, columns(g)], 1, 0)
        return own + dot(xm_ref[z], gm_ref[:, columns(g)], 1, 0)

    def partial_extra(z, g):
        return partial(z, g) + dot(xe_ref[z], ge_ref[:, columns(g)], 1, 0)

    def term(z, g):
        down = (z < me).astype(jnp.int32)
        to = me + 1 - 2 * down
        slot = jnp.where((down == 1) & (to == z), n, z)
        return pltpu.make_async_remote_copy(
            src_ref=st_ref.at[z, g], dst_ref=st_ref.at[slot, g],
            send_sem=ss.at[z, g], recv_sem=rs.at[slot, g],
            device_id={"seq": to}, device_id_type=MESH,
        )

    def arrived(slot, g):
        pltpu.make_async_remote_copy(
            src_ref=st_ref.at[slot, g], dst_ref=st_ref.at[slot, g],
            send_sem=ss.at[0, g], recv_sem=rs.at[slot, g],
            device_id={"dp": mate}, device_id_type=MESH,
        ).wait_recv()

    def wait_x():
        @pl.when(inside)
        def _():
            lax.fori_loop(0, n, lambda z, c: (x_copy(z).wait_recv(), c)[1], 0)

        @pl.when(is_end)
        def _():
            x_copy(far(n - 1)).wait_recv()

    def take_factor(g):
        @pl.when(is_hub)
        def _():
            ends_copy(g).wait_recv()
            pass_copy(g).start()

    def send_far(g):
        gk_copy(g).wait_recv()

        @pl.when(is_hub)
        def _():
            pass_copy(g).wait_recv()

            def one(e):
                z = far(e)
                pl.when(g == 0)(lambda: have_early(e, 1))
                st_ref[z, g] = partial_extra(z, g).astype(BF16)
                term(z, g).start()

            repeat(late, one)

    def pass_on(z, g):
        total = partial(z, g)
        arrived(z, g)
        st_ref[z, g] = (total + st_ref[z, g].astype(F32)).astype(BF16)
        term(z, g).start()

    def send_on(g):
        pl.when(is_hub)(lambda: pass_on(ext, g))
        if n > 4:
            @pl.when(jnp.logical_not(is_hub | is_end))
            def _():
                def step(j, c):
                    z = (j // 2) * (1 - j % 2) + (n - 1 - j // 2) * (j % 2)
                    pl.when(z != me)(lambda: pass_on(z, g))
                    return c
                lax.fori_loop(0, n, step, 0)

    def guarded(cond, body):
        pl.when(cond)(body)

    greeted()
    update(0)
    update(1)
    make_mask()
    turn_inputs()
    send_early(0, lead)
    relay_forward(0)

    def iteration(i, c):
        guarded(i + 1 < groups, lambda: relay_forward(i + 1))
        guarded(i + 2 < groups, lambda: update(i + 2))

        @pl.when(i < groups)
        def _():
            scores(i)
            attend(i)

        last = jnp.where(2 * me >= n, 1, 2)
        guarded((i >= last) & (i - last < groups), lambda: relay_back(i - last))
        guarded(i == 1, lambda: send_early(lead, late))
        guarded(i == groups, lambda: send_early(late, late + 1))
        guarded((i >= 2) & (i - 2 < groups), lambda: finish(i - 2))
        guarded(i == 3, lambda: take_early(0, lead))
        guarded(i == 5, lambda: take_early(lead, late))
        guarded(i == 5, wait_x)
        guarded((i >= LAG) & (i - LAG < groups), lambda: take_factor(i - LAG))
        guarded(i < groups, lambda: grads(i))
        guarded((i >= LAG) & (i - LAG < groups), lambda: send_far(i - LAG))
        guarded((i >= LAG + 1) & (i - LAG - 1 < groups), lambda: send_on(i - LAG - 1))
        guarded(i == LAG + 4, lambda: take_early(late, late + 1))
        return c

    lax.fori_loop(0, max(groups, 4) + LAG + 1, iteration, 0)

    def settle(g):
        @pl.when(is_hub)
        def _():
            pl.when(g == 0)(lambda: have_early(late, 1))
            out_ref[:, columns(g)] = partial_extra(me, g)

        @pl.when(jnp.logical_not(is_hub))
        def _():
            out_ref[:, columns(g)] = partial(me, g)

        @pl.when(me > 1)
        def _():
            arrived(me, g)
            out_ref[:, columns(g)] += st_ref[me, g].astype(F32)

        @pl.when(me < n - 2)
        def _():
            arrived(n, g)
            out_ref[:, columns(g)] += st_ref[n, g].astype(F32)

        store(2, g).start()

    each_group(settle)

    def drain(g):
        @pl.when(me < n - 1)
        def _():
            forward(g).wait_send()

        @pl.when(me > 0)
        def _():
            backward(g).wait_send()

        gk_copy(g).wait_send()
        pl.when(is_end)(lambda: ends_copy(g).wait_send())
        pl.when(is_hub)(lambda: pass_copy(g).wait_send())
        for a in range(3):
            store(a, g).wait()

        @pl.when(inside)
        def _():
            def step(z, c):
                pl.when(z != me)(lambda: term(z, g).wait_send())
                return c
            lax.fori_loop(0, n, step, 0)

    each_group(drain)

    def sent_x(z, c):
        x_copy(z).wait_send()
        return c

    lax.fori_loop(0, n, sent_x, 0)

    def sent_early(e, c):
        for part in range(2):
            pl.when(is_end)(lambda: early_copy(e, part).wait_send())
            if paired:
                pl.when(is_hub)(lambda: pair_copy(e, part, side).wait_send())
        return c

    lax.fori_loop(0, n - 1, sent_early, 0)


def layer(lengths, log_decay, x, q, k, v, g):
    heads, B = log_decay.shape
    D, F = x.shape[1], q.shape[1]
    n, group, groups, rows = sizes(heads, D)
    hbm = pl.BlockSpec(memory_space=pl.ANY)
    state = (heads, LANES, LANES)
    wide = jax.ShapeDtypeStruct((B, F), BF16)
    dma = pltpu.SemaphoreType.DMA
    return pl.pallas_call(
        functools.partial(layer_kernel, heads),
        out_shape=(wide, wide, jax.ShapeDtypeStruct((rows, F), F32)),
        in_specs=[
            pl.BlockSpec(memory_space=pltpu.SMEM), pl.BlockSpec(memory_space=pltpu.VMEM)
        ] + [hbm] * 5,
        out_specs=(hbm, hbm, hbm),
        scratch_shapes=[pltpu.VMEM((B, F), BF16)] * 4
        + [
            pltpu.VMEM((B, D), BF16),
            pltpu.VMEM((D, B), BF16),
            pltpu.VMEM((n, rows, B), BF16),
            pltpu.VMEM((n, rows, 2 * B), BF16),
            pltpu.VMEM((B, F), BF16),
            pltpu.VMEM((2 * B, F), BF16),
            pltpu.VMEM((n + 1, groups, rows, group * LANES), BF16),
            pltpu.VMEM((rows, F), F32),
            pltpu.VMEM((heads, B), F32),
            pltpu.VMEM((heads, B, LANES), F32),
            pltpu.VMEM((B, B), F32),
            pltpu.VMEM((B, LANES), F32),
            pltpu.VMEM((B, LANES), F32),
            pltpu.VMEM(state, F32),
            pltpu.VMEM((group, B, LANES), F32),
            pltpu.VMEM((group, B, B), BF16),
            pltpu.VMEM((group, B, LANES), BF16),
            pltpu.VMEM(state, F32),
            pltpu.VMEM((2 * group, B, LANES), F32),
            pltpu.VMEM((2 * group, B, LANES), F32),
        ]
        + [pltpu.VMEM(state, BF16)] * 4
        + [dma((groups,))] * 4
        + [
            dma((4, groups)), dma(()), dma((3, groups)), dma((n,)), dma((n,)),
            dma((groups,)), dma((groups,)), dma((n, groups)), dma((n + 1, groups)),
        ]
        + [dma((n, 2))] * 4 + [dma((groups,))] * 4,
        compiler_params=pltpu.CompilerParams(
            collective_id=0, has_side_effects=True, vmem_limit_bytes=62 * 1024 * 1024
        ),
        name="layer",
    )(lengths, log_decay, x, q, k, v, g)


def deliver_kernel(pieces, *refs):
    count = (len(refs) - 2) // 3
    srcs, dsts, bufs = refs[:count], refs[count : 2 * count], refs[2 * count : 3 * count]
    in_sem, out_sem = refs[3 * count :]
    spans = []
    for a in range(count):
        size = srcs[a].shape[0] // pieces
        spans += [(a, p, pl.ds(p * size, size)) for p in range(pieces)]

    def load(a, p, span):
        return pltpu.make_async_copy(srcs[a].at[span], bufs[a].at[span], in_sem.at[a, p])

    def store(a, p, span):
        return pltpu.make_async_copy(bufs[a].at[span], dsts[a].at[span], out_sem.at[a, p])

    for item in spans:
        load(*item).start()
    for item in spans:
        load(*item).wait()
        store(*item).start()
    for item in spans:
        store(*item).wait()


def deliver(*arrays):
    pieces = 4
    hbm = pl.BlockSpec(memory_space=pl.ANY)
    sems = pltpu.SemaphoreType.DMA((len(arrays), pieces))
    return pl.pallas_call(
        functools.partial(deliver_kernel, pieces),
        out_shape=tuple(jax.ShapeDtypeStruct(a.shape, a.dtype) for a in arrays),
        in_specs=[hbm] * len(arrays),
        out_specs=(hbm,) * len(arrays),
        scratch_shapes=[pltpu.VMEM(a.shape, a.dtype) for a in arrays] + [sems, sems],
        compiler_params=pltpu.CompilerParams(vmem_limit_bytes=60 * 1024 * 1024),
        name="deliver",
    )(*arrays)


def body(inputs, queries, keys, values, log_decay, list_lengths, grad_out):
    gq, gv, gw = layer(
        list_lengths, log_decay[0], inputs[0], queries[0], keys[0], values[0], grad_out[0]
    )
    gq, gv, gw = deliver(gq, gv, gw)
    return gq[None], gv[None], gw


def solution(mesh):
    rows = ("groups", "dp")
    wide = P(rows, "seq", "head")
    return jax.shard_map(
        body,
        mesh=mesh,
        in_specs=(
            P(rows, "seq", None), wide, wide, wide, P(rows, "head", "seq"), P(rows, None), wide,
        ),
        out_specs=(wide, wide, P(("groups", "seq", "dp"), "head")),
        check_vma=False,
    )
```

```python
import functools
import math

import jax
import jax.numpy as jnp
from jax import lax
from jax.experimental import pallas as pl
from jax.experimental.pallas import tpu as pltpu
from jax.sharding import PartitionSpec as P

EPS = 1e-06
MESH = pl.DeviceIdType.MESH
LANES = 128
F32 = jnp.float32
BF16 = jnp.bfloat16


def dot(a, b, ca, cb):
    return lax.dot_general(a, b, (((ca,), (cb,)), ((), ())), preferred_element_type=F32)


def greet(pair):
    barrier = pltpu.get_barrier_semaphore()
    me = lax.axis_index("seq")
    n = lax.axis_size("seq")

    @pl.when(me > 0)
    def _():
        pl.semaphore_signal(barrier, inc=1, device_id={"seq": me - 1}, device_id_type=MESH)

    @pl.when(me < n - 1)
    def _():
        pl.semaphore_signal(barrier, inc=1, device_id={"seq": me + 1}, device_id_type=MESH)

    peers = (me > 0).astype(jnp.int32) + (me < n - 1).astype(jnp.int32) + 1
    mate = 1 - lax.axis_index("dp")
    pl.semaphore_signal(barrier, inc=1, device_id={"dp": mate}, device_id_type=MESH)
    if pair is not None:
        pl.semaphore_signal(barrier, inc=1, device_id={"head": pair}, device_id_type=MESH)
        peers = peers + 1
    return lambda: pl.semaphore_wait(barrier, peers)


def sizes(heads, D):
    group = math.gcd(heads, 2)
    n = lax.axis_size("seq")
    return n, group, heads // group, D // (2 * n)


def repeat(count, body):
    if count <= 3:
        for i in range(count):
            body(i)
        return

    def step(i, c):
        body(i)
        return c

    lax.fori_loop(0, count, step, 0)


def layer_kernel(
    heads, ll_ref, ld_ref, x_hbm, q_hbm, k_hbm, v_hbm, g_hbm, q_ref, g_ref, out_ref,
    k_ref, v_ref, x_ref, xt_ref, xm_ref, xe_ref, gm_ref, ge_ref, st_ref,
    cum_ref, colb_ref, mask_ref, min_ref, mout_ref, upd_ref, sc_ref, ga_ref,
    bs_ref, fsend, frecv, bsend, brecv, fss, frs, bss, brs,
    load_sem, x_sem, xss, xrs, gss, grs, ss, rs, ess, ers, pss, prs, hss, hrs, mss, mrs,
):
    me = lax.axis_index("seq")
    dp = lax.axis_index("dp")
    hx = lax.axis_index("head")
    B, D = x_ref.shape
    n, group, groups, rows = sizes(heads, D)
    first = me * B
    mate = 1 - dp
    width = group * LANES
    paired = lax.axis_size("head") % 2 == 0
    half = rows // 2 if paired else rows
    side = hx % 2 if paired else 0
    pair = hx + 1 - 2 * side if paired else None
    late = n - 2

    is_end = (me == 0) | (me == n - 1)
    is_hub = (me == 1) | (me == n - 2)
    inside = jnp.logical_not(is_end)
    low = me <= 1
    hub = jnp.where(low, 1, n - 2)
    ext = jnp.where(low, 0, n - 1)

    def far(e):
        return jnp.where(low, n - 1 - e, e)

    def columns(g):
        return pl.ds(pl.multiple_of(g * width, LANES), width)

    def load(a, part):
        src = (k_hbm, v_hbm, q_hbm, g_hbm)[a]
        dst = (k_ref, v_ref, q_ref, g_ref)[a]
        cols = (slice(0, width), slice(width, heads * LANES), slice(0, heads * LANES))[part]
        return pltpu.make_async_copy(src.at[:, cols], dst.at[:, cols], load_sem.at[a, min(part, 1)])

    def each_group(body, start=0):
        def step(g, c):
            body(g)
            return c
        lax.fori_loop(start, groups, step, 0)

    greeted = greet(pair)

    load_x = pltpu.make_async_copy(x_hbm, x_ref, x_sem)
    upper = 2 * me >= n
    pl.when(upper)(load_x.start)
    for a in range(2):
        load(a, 0).start()
    pl.when(jnp.logical_not(upper))(load_x.start)
    for a in range(2):
        load(a, 1).start()

    lengths = [ll_ref[0, i] for i in range(ll_ref.shape[1])]
    starts = [jnp.int32(0)]
    for length in lengths[:-1]:
        starts.append(starts[-1] + length)

    def seg_of(pos):
        total = (starts[0] <= pos).astype(jnp.int32)
        for s in starts[1:]:
            total = total + (s <= pos).astype(jnp.int32)
        return total

    before = seg_of(first - 1)
    end = seg_of(first + B - 1)
    seg_col = seg_of(first + lax.broadcasted_iota(jnp.int32, (B, LANES), 0))
    min_ref[...] = jnp.where(seg_col == before, 1.0, 0.0).astype(F32)
    mout_ref[...] = jnp.where(seg_col == end, 1.0, 0.0).astype(F32)
    open_all = jnp.where(jnp.full((1, LANES), end) == before, 1.0, 0.0).astype(F32)
    above = lax.broadcasted_iota(jnp.int32, (LANES, LANES), 0)
    below = lax.broadcasted_iota(jnp.int32, (LANES, LANES), 1)
    tri = jnp.where(above <= below, 1.0, 0.0).astype(F32)
    carry = jnp.zeros((heads, 1), F32)
    for c in range(B // LANES):
        span = slice(c * LANES, (c + 1) * LANES)
        run = carry + lax.dot_general(
            ld_ref[:, span], tri, (((1,), (0,)), ((), ())),
            preferred_element_type=F32, precision=lax.Precision.HIGHEST,
        )
        cum_ref[:, span] = run
        carry = run[:, LANES - 1 :]

    def make_mask():
        t_pos = lax.broadcasted_iota(jnp.int32, (B, B), 0)
        u_pos = lax.broadcasted_iota(jnp.int32, (B, B), 1)
        wide = jnp.concatenate([seg_col] * (B // LANES), axis=1)
        row = seg_of(first + lax.broadcasted_iota(jnp.int32, (1, B), 1))
        same = (t_pos >= u_pos) & (wide == row)
        mask_ref[...] = jnp.where(same, 0.0, -1e30).astype(F32)

    def lanes(h):
        return pl.ds(pl.multiple_of(h * LANES, LANES), LANES)

    def weight_of(h):
        cb = colb_ref[h]
        return jnp.exp(cb[B - 1 : B, :] - cb) * mout_ref[...]

    def gamma_of(h):
        return jnp.exp(colb_ref[h]) * min_ref[...]

    def passing_of(h):
        return jnp.exp(colb_ref[h, B - 1 : B, :]) * open_all

    def decay_of(h, ts, cols):
        cb = colb_ref[h, ts, :]
        wide = jnp.concatenate([cb] * (cols // LANES), axis=1)
        row = cum_ref[pl.ds(h, 1), :cols]
        return jnp.exp((wide - row) + mask_ref[ts, :cols])

    def each_head(g, body):
        for i in range(group):
            body(g * group + i, i)

    def hop(src, dst, ss, rs, g, to):
        span = pl.ds(g * group, group)
        return pltpu.make_async_remote_copy(
            src_ref=src.at[span], dst_ref=dst.at[span], send_sem=ss.at[g], recv_sem=rs.at[g],
            device_id={"seq": to}, device_id_type=MESH,
        )

    def forward(g):
        return hop(fsend, frecv, fss, frs, g, me + 1)

    def backward(g):
        return hop(bsend, brecv, bss, brs, g, me - 1)

    def update(g):
        for part in range(2):
            @pl.when(g == part)
            def _():
                load(0, part).wait()
                load(1, part).wait()

        def column(h, i):
            colb_ref[h] = jnp.transpose(jnp.broadcast_to(cum_ref[pl.ds(h, 1), :], (LANES, B)))

        def one(h, i):
            column(h, i)
            wk = (k_ref[:, lanes(h)].astype(F32) * weight_of(h)).astype(BF16)
            upd_ref[h] = dot(wk, v_ref[:, lanes(h)], 0, 0)

        pl.when(me == n - 1)(lambda: each_head(g, column))
        pl.when(me < n - 1)(lambda: each_head(g, one))

        @pl.when(me == 0)
        def _():
            def ready(h, i):
                fsend[h] = upd_ref[h].astype(BF16)
                frecv[h] = jnp.zeros((LANES, LANES), BF16)
            each_head(g, ready)
            forward(g).start()

        @pl.when(me == n - 1)
        def _():
            def ready(h, i):
                brecv[h] = jnp.zeros((LANES, LANES), BF16)
            each_head(g, ready)

    def relay_forward(g):
        @pl.when(inside)
        def _():
            forward(g).wait_recv()

            def send(h, i):
                fsend[h] = (passing_of(h) * frecv[h].astype(F32) + upd_ref[h]).astype(BF16)
            each_head(g, send)
            forward(g).start()

    def attention(g):
        @pl.when(g == 0)
        def _():
            load(2, 2).wait()
            load(3, 2).wait()

        @pl.when(me == n - 1)
        def _():
            forward(g).wait_recv()

        def one(h, i):
            q = q_ref[:, lanes(h)]
            s = dot(q, k_ref[:, lanes(h)], 1, 1)
            s_bf = (s * decay_of(h, slice(0, B), B)).astype(BF16)
            sc_ref[h] = s_bf
            gamma = gamma_of(h)
            att = gamma * dot(q, frecv[h], 1, 0) + dot(s_bf, v_ref[:, lanes(h)], 1, 0)
            inv = lax.rsqrt(jnp.mean(att * att, axis=-1, keepdims=True) + EPS)
            normed = att * inv
            wide = g_ref[:, lanes(h)].astype(F32)
            ga = (inv * (wide - normed * jnp.mean(wide * normed, axis=-1, keepdims=True))).astype(BF16)
            ga_ref[h] = ga
            gated = (q.astype(F32) * gamma).astype(BF16)
            bs_ref[h] = dot(gated, ga, 0, 0)

        each_head(g, one)

        @pl.when(me == n - 1)
        def _():
            def ready(h, i):
                bsend[h] = bs_ref[h].astype(BF16)
            each_head(g, ready)
            backward(g).start()

    def relay_back(g):
        @pl.when(me < n - 1)
        def _():
            backward(g).wait_recv()

        @pl.when(inside)
        def _():
            def send(h, i):
                bsend[h] = (passing_of(h) * brecv[h].astype(F32) + bs_ref[h]).astype(BF16)
            each_head(g, send)
            backward(g).start()

    tile = math.gcd(B, 256)
    tiles = B // tile

    def grads(g):
        def one(h, i):
            gamma = gamma_of(h)
            w = weight_of(h)
            later = brecv[h]
            kis, vis = [None] * tiles, [None] * tiles
            for b in range(tiles):
                ts, cols = slice(b * tile, (b + 1) * tile), (b + 1) * tile
                ga = ga_ref[h, ts, :]
                q = q_ref[ts, lanes(h)]
                gs = (dot(ga, v_ref[:cols, lanes(h)], 1, 1) * decay_of(h, ts, cols)).astype(BF16)
                gq = gamma[ts] * dot(ga, frecv[h], 1, 1) + dot(gs, k_ref[:cols, lanes(h)], 1, 0)
                ki = dot(gs, q, 0, 0)
                vi = dot(sc_ref[h, ts, :cols], ga, 0, 0)
                q_ref[ts, lanes(h)] = gq.astype(BF16)
                for j in range(b + 1):
                    js = slice(j * tile, (j + 1) * tile)
                    kis[j] = ki[js] if kis[j] is None else kis[j] + ki[js]
                    vis[j] = vi[js] if vis[j] is None else vis[j] + vi[js]
            for j in range(tiles):
                js = slice(j * tile, (j + 1) * tile)
                k = k_ref[js, lanes(h)]
                gk = kis[j] + w[js] * dot(v_ref[js, lanes(h)], later, 1, 1)
                gv = vis[j] + w[js] * dot(k, later, 1, 0)
                k_ref[js, lanes(h)] = gk.astype(BF16)
                g_ref[js, lanes(h)] = gv.astype(BF16)

        each_head(g, one)
        pl.when(is_end)(lambda: ends_copy(g).start())
        gk_copy(g).start()

    def gk_copy(g):
        return pltpu.make_async_remote_copy(
            src_ref=k_ref.at[:, columns(g)], dst_ref=gm_ref.at[:, columns(g)],
            send_sem=gss.at[g], recv_sem=grs.at[g],
            device_id={"dp": mate}, device_id_type=MESH,
        )

    def ends_copy(g):
        return pltpu.make_async_remote_copy(
            src_ref=k_ref.at[:, columns(g)], dst_ref=ge_ref.at[pl.ds(0, B), columns(g)],
            send_sem=hss.at[g], recv_sem=hrs.at[g],
            device_id={"seq": hub}, device_id_type=MESH,
        )

    def pass_copy(g):
        return pltpu.make_async_remote_copy(
            src_ref=ge_ref.at[pl.ds(0, B), columns(g)], dst_ref=ge_ref.at[pl.ds(B, B), columns(g)],
            send_sem=mss.at[g], recv_sem=mrs.at[g],
            device_id={"dp": mate}, device_id_type=MESH,
        )

    def share(z, owner):
        return pl.ds(pl.multiple_of((z * 2 + owner) * rows, math.gcd(rows, LANES)), rows)

    def halves(which, base=0):
        return pl.ds(pl.multiple_of(base + which * half, math.gcd(half, LANES)), half)

    def x_copy(z):
        return pltpu.make_async_remote_copy(
            src_ref=xt_ref.at[share(z, mate)], dst_ref=xm_ref.at[z],
            send_sem=xss.at[z], recv_sem=xrs.at[z],
            device_id={"dp": mate}, device_id_type=MESH,
        )

    def turn(i, c):
        span = pl.ds(pl.multiple_of(i * LANES, LANES), LANES)
        xt_ref[span, :] = jnp.transpose(x_ref[:, span])
        return c

    def turn_inputs():
        load_x.wait()
        lax.fori_loop(0, D // LANES, turn, 0)

    def swap_inputs():
        lax.fori_loop(0, n, lambda e, c: (x_copy(far(e)).start(), c)[1], 0)

    def early_copy(e, part):
        z = far(e)
        src = (
            xt_ref.at[halves(side, (z * 2 + dp) * rows)] if part == 0 else xm_ref.at[z, halves(side)]
        )
        return pltpu.make_async_remote_copy(
            src_ref=src, dst_ref=xe_ref.at[z, halves(side), pl.ds(part * B, B)],
            send_sem=ess.at[z, part], recv_sem=ers.at[z, part],
            device_id={"seq": hub}, device_id_type=MESH,
        )

    def pair_copy(e, part, which):
        z = far(e)
        ref = xe_ref.at[z, halves(which), pl.ds(part * B, B)]
        return pltpu.make_async_remote_copy(
            src_ref=ref, dst_ref=ref, send_sem=pss.at[z, part], recv_sem=prs.at[z, part],
            device_id={"head": pair}, device_id_type=MESH,
        )

    def send_early(lo, hi):
        for j in range(lo, hi):
            if j % 2 == 1:
                x_copy(far(j // 2)).wait_recv()
            early_copy(j // 2, j % 2).start()

    def take_early(lo, hi):
        for j in range(lo, hi):
            early_copy(j // 2, j % 2).wait_recv()
            if paired:
                pair_copy(j // 2, j % 2, side).start()

    def have_early(lo, count):
        if paired:
            def one(e):
                for part in range(2):
                    pair_copy(lo + e, part, 1 - side).wait_recv()
            repeat(count, one)

    def partial(z, g):
        own = dot(xt_ref[share(z, dp), :], k_ref[:, columns(g)], 1, 0)
        return own + dot(xm_ref[z], gm_ref[:, columns(g)], 1, 0)

    def partial_extra(z, g):
        return partial(z, g) + dot(xe_ref[z], ge_ref[:, columns(g)], 1, 0)

    def term(z, g):
        down = (z < me).astype(jnp.int32)
        to = me + 1 - 2 * down
        slot = jnp.where((down == 1) & (to == z), n, z)
        return pltpu.make_async_remote_copy(
            src_ref=st_ref.at[z, g], dst_ref=st_ref.at[slot, g],
            send_sem=ss.at[z, g], recv_sem=rs.at[slot, g],
            device_id={"seq": to}, device_id_type=MESH,
        )

    def arrived(slot, g):
        pltpu.make_async_remote_copy(
            src_ref=st_ref.at[slot, g], dst_ref=st_ref.at[slot, g],
            send_sem=ss.at[0, g], recv_sem=rs.at[slot, g],
            device_id={"dp": mate}, device_id_type=MESH,
        ).wait_recv()

    def wait_x():
        @pl.when(inside)
        def _():
            lax.fori_loop(0, n, lambda z, c: (x_copy(z).wait_recv(), c)[1], 0)

        @pl.when(is_end)
        def _():
            x_copy(far(n - 1)).wait_recv()

    def take_factor(g):
        @pl.when(is_hub)
        def _():
            ends_copy(g).wait_recv()
            pass_copy(g).start()

    def send_far(g):
        gk_copy(g).wait_recv()

        @pl.when(is_hub)
        def _():
            pass_copy(g).wait_recv()

            def one(e):
                z = far(e)
                pl.when(g == 0)(lambda: have_early(e, 1))
                st_ref[z, g] = partial_extra(z, g).astype(BF16)
                term(z, g).start()

            repeat(late, one)

    def pass_on(z, g):
        total = partial(z, g)
        arrived(z, g)
        st_ref[z, g] = (total + st_ref[z, g].astype(F32)).astype(BF16)
        term(z, g).start()

    def send_on(g):
        pl.when(is_hub)(lambda: pass_on(ext, g))
        if n > 4:
            @pl.when(jnp.logical_not(is_hub | is_end))
            def _():
                def step(j, c):
                    z = (j // 2) * (1 - j % 2) + (n - 1 - j // 2) * (j % 2)
                    pl.when(z != me)(lambda: pass_on(z, g))
                    return c
                lax.fori_loop(0, n, step, 0)

    def guarded(cond, body):
        pl.when(cond)(body)

    pieces = 2 * late
    most = pieces // 2
    pl.when(upper)(turn_inputs)
    greeted()
    for a in range(2, 4):
        load(a, 2).start()
    pl.when(upper)(swap_inputs)
    pl.when(me == n - 1)(lambda: send_early(0, most))

    ahead = min(groups, 4)

    def prepare(g):
        update(g)
        guarded(g >= ahead, lambda: relay_forward(g - ahead))

    each_group(prepare)
    make_mask()

    @pl.when(me == 0)
    def _():
        turn_inputs()
        swap_inputs()
        send_early(0, pieces)

    behind = jnp.where(me == 0, groups - 1, jnp.minimum((n - 2 - me) * 3, groups - 1))
    products = groups + 2

    def iteration(i, c):
        done = i - groups
        guarded(i < ahead, lambda: relay_forward(i + groups - ahead))
        guarded(i < groups, lambda: attention(i))

        @pl.when(inside & jnp.logical_not(upper) & (i == groups))
        def _():
            turn_inputs()
            swap_inputs()

        for q in range(3):
            lo, hi = pieces * q // 4, pieces * (q + 1) // 4
            at = max(0, groups - 4 + 2 * q)
            guarded(is_hub & (i == at), lambda: take_early(lo, hi))
        split = (most + pieces) // 2
        guarded((me == n - 1) & (i == groups // 2 - 1), lambda: send_early(most, split))
        guarded((me == n - 1) & (i == groups - 2), lambda: send_early(split, pieces))
        guarded(is_end & (done == 5), lambda: send_early(pieces, pieces + 2))
        guarded((done >= 0) & (done < groups), lambda: grads(done))
        guarded(is_hub & (done == 1), lambda: take_early(pieces * 3 // 4, pieces))

        guarded(i == products, wait_x)

        ready = i - products
        guarded((ready >= 0) & (ready < groups), lambda: take_factor(ready))
        guarded((ready >= 0) & (ready < groups), lambda: send_far(ready))
        guarded((ready >= 1) & (ready - 1 < groups), lambda: send_on(ready - 1))
        guarded(is_hub & (ready == 6), lambda: take_early(pieces, pieces + 2))
        guarded((i >= behind) & (i - behind < groups), lambda: relay_back(i - behind))
        return c

    lax.fori_loop(0, products + max(groups, 6) + 1, iteration, 0)

    def settle(g):
        @pl.when(is_hub)
        def _():
            pl.when(g == 0)(lambda: have_early(late, 1))
            out_ref[:, columns(g)] = partial_extra(me, g)

        @pl.when(jnp.logical_not(is_hub))
        def _():
            out_ref[:, columns(g)] = partial(me, g)

        @pl.when(me > 1)
        def _():
            arrived(me, g)
            out_ref[:, columns(g)] += st_ref[me, g].astype(F32)

        @pl.when(me < n - 2)
        def _():
            arrived(n, g)
            out_ref[:, columns(g)] += st_ref[n, g].astype(F32)

    each_group(settle)

    def drain(g):
        @pl.when(me < n - 1)
        def _():
            forward(g).wait_send()

        @pl.when(me > 0)
        def _():
            backward(g).wait_send()

        gk_copy(g).wait_send()
        pl.when(is_end)(lambda: ends_copy(g).wait_send())
        pl.when(is_hub)(lambda: pass_copy(g).wait_send())

        @pl.when(inside)
        def _():
            def step(z, c):
                pl.when(z != me)(lambda: term(z, g).wait_send())
                return c
            lax.fori_loop(0, n, step, 0)

    each_group(drain)

    def sent_x(z, c):
        x_copy(z).wait_send()
        return c

    lax.fori_loop(0, n, sent_x, 0)

    def sent_early(e, c):
        for part in range(2):
            pl.when(is_end)(lambda: early_copy(e, part).wait_send())
            if paired:
                pl.when(is_hub)(lambda: pair_copy(e, part, side).wait_send())
        return c

    lax.fori_loop(0, n - 1, sent_early, 0)


def layer(lengths, log_decay, x, q, k, v, g):
    heads, B = log_decay.shape
    D, F = x.shape[1], q.shape[1]
    n, group, groups, rows = sizes(heads, D)
    hbm = pl.BlockSpec(memory_space=pl.ANY)
    vmem = pl.BlockSpec(memory_space=pltpu.VMEM)
    state = (heads, LANES, LANES)
    wide = pltpu.VMEM((B, F), BF16)
    dma = pltpu.SemaphoreType.DMA
    return pl.pallas_call(
        functools.partial(layer_kernel, heads),
        out_shape=(wide, wide, pltpu.VMEM((rows, F), F32)),
        in_specs=[
            pl.BlockSpec(memory_space=pltpu.SMEM), pl.BlockSpec(memory_space=pltpu.VMEM)
        ] + [hbm] * 5,
        out_specs=(vmem, vmem, vmem),
        scratch_shapes=[pltpu.VMEM((B, F), BF16)] * 2
        + [
            pltpu.VMEM((B, D), BF16),
            pltpu.VMEM((D, B), BF16),
            pltpu.VMEM((n, rows, B), BF16),
            pltpu.VMEM((n, rows, 2 * B), BF16),
            pltpu.VMEM((B, F), BF16),
            pltpu.VMEM((2 * B, F), BF16),
            pltpu.VMEM((n + 1, groups, rows, group * LANES), BF16),
            pltpu.VMEM((heads, B), F32),
            pltpu.VMEM((heads, B, LANES), F32),
            pltpu.VMEM((B, B), F32),
            pltpu.VMEM((B, LANES), F32),
            pltpu.VMEM((B, LANES), F32),
            pltpu.VMEM(state, F32),
            pltpu.VMEM((heads, B, B), BF16),
            pltpu.VMEM((heads, B, LANES), BF16),
            pltpu.VMEM(state, F32),
        ]
        + [pltpu.VMEM(state, BF16)] * 4
        + [dma((groups,))] * 4
        + [
            dma((4, 2)), dma(()), dma((n,)), dma((n,)),
            dma((groups,)), dma((groups,)), dma((n, groups)), dma((n + 1, groups)),
        ]
        + [dma((n, 2))] * 4 + [dma((groups,))] * 4,
        compiler_params=pltpu.CompilerParams(
            collective_id=0, has_side_effects=True, vmem_limit_bytes=55 * 1024 * 1024
        ),
        name="layer",
    )(lengths, log_decay, x, q, k, v, g)


def deliver_kernel(*refs):
    count = (len(refs) - 1) // 2
    srcs, dsts, sem = refs[:count], refs[count:-1], refs[-1]
    moves = [pltpu.make_async_copy(srcs[a], dsts[a], sem.at[a]) for a in range(count)]
    for move in moves:
        move.start()
    for move in moves:
        move.wait()


def deliver(*arrays):
    hbm = pl.BlockSpec(memory_space=pl.ANY)
    vmem = pl.BlockSpec(memory_space=pltpu.VMEM)
    return pl.pallas_call(
        deliver_kernel,
        out_shape=tuple(jax.ShapeDtypeStruct(a.shape, a.dtype) for a in arrays),
        in_specs=[vmem] * len(arrays),
        out_specs=(hbm,) * len(arrays),
        scratch_shapes=[pltpu.SemaphoreType.DMA((len(arrays),))],
        compiler_params=pltpu.CompilerParams(vmem_limit_bytes=16 * 1024 * 1024),
        name="deliver",
    )(*arrays)


def body(inputs, queries, keys, values, log_decay, list_lengths, grad_out):
    gq, gv, gw = layer(
        list_lengths, log_decay[0], inputs[0], queries[0], keys[0], values[0], grad_out[0]
    )
    gq, gv, gw = deliver(gq, gv, gw)
    return gq[None], gv[None], gw


def solution(mesh):
    rows = ("groups", "dp")
    wide = P(rows, "seq", "head")
    return jax.shard_map(
        body,
        mesh=mesh,
        in_specs=(
            P(rows, "seq", None), wide, wide, wide, P(rows, "head", "seq"), P(rows, None), wide,
        ),
        out_specs=(wide, wide, P(("groups", "seq", "dp"), "head")),
        check_vma=False,
    )
```

```python
import functools
import math

import jax
import jax.numpy as jnp
from jax import lax
from jax.experimental import pallas as pl
from jax.experimental.pallas import tpu as pltpu
from jax.sharding import PartitionSpec as P

EPS = 1e-06
MESH = pl.DeviceIdType.MESH
LANES = 128
F32 = jnp.float32
BF16 = jnp.bfloat16


def dot(a, b, ca, cb):
    return lax.dot_general(a, b, (((ca,), (cb,)), ((), ())), preferred_element_type=F32)


def greet(pair):
    barrier = pltpu.get_barrier_semaphore()
    me = lax.axis_index("seq")
    n = lax.axis_size("seq")

    @pl.when(me > 0)
    def _():
        pl.semaphore_signal(barrier, inc=1, device_id={"seq": me - 1}, device_id_type=MESH)

    @pl.when(me < n - 1)
    def _():
        pl.semaphore_signal(barrier, inc=1, device_id={"seq": me + 1}, device_id_type=MESH)

    peers = (me > 0).astype(jnp.int32) + (me < n - 1).astype(jnp.int32) + 1
    mate = 1 - lax.axis_index("dp")
    pl.semaphore_signal(barrier, inc=1, device_id={"dp": mate}, device_id_type=MESH)
    if pair is not None:
        pl.semaphore_signal(barrier, inc=1, device_id={"head": pair}, device_id_type=MESH)
        peers = peers + 1
    return lambda: pl.semaphore_wait(barrier, peers)


def sizes(heads, D):
    group = math.gcd(heads, 2)
    n = lax.axis_size("seq")
    return n, group, heads // group, D // (2 * n)


def repeat(count, body):
    if count <= 3:
        for i in range(count):
            body(i)
        return

    def step(i, c):
        body(i)
        return c

    lax.fori_loop(0, count, step, 0)


def layer_kernel(
    heads, ll_ref, ld_ref, x_hbm, q_hbm, k_hbm, v_hbm, g_hbm, q_ref, g_ref, out_ref,
    k_ref, v_ref, x_ref, xt_ref, xm_ref, xe_ref, gm_ref, ge_ref, st_ref,
    cum_ref, colb_ref, mask_ref, min_ref, mout_ref, upd_ref, sc_ref, ga_ref,
    bs_ref, fsend, frecv, bsend, brecv, fss, frs, bss, brs,
    load_sem, x_sem, xss, xrs, gss, grs, ss, rs, ess, ers, pss, prs, hss, hrs, mss, mrs,
):
    me = lax.axis_index("seq")
    dp = lax.axis_index("dp")
    hx = lax.axis_index("head")
    B, D = x_ref.shape
    n, group, groups, rows = sizes(heads, D)
    first = me * B
    mate = 1 - dp
    width = group * LANES
    paired = lax.axis_size("head") % 2 == 0
    half = rows // 2 if paired else rows
    side = hx % 2 if paired else 0
    pair = hx + 1 - 2 * side if paired else None
    late = n - 2

    is_end = (me == 0) | (me == n - 1)
    is_hub = (me == 1) | (me == n - 2)
    inside = jnp.logical_not(is_end)
    low = me <= 1
    hub = jnp.where(low, 1, n - 2)
    ext = jnp.where(low, 0, n - 1)

    def far(e):
        return jnp.where(low, n - 1 - e, e)

    def columns(g):
        return pl.ds(pl.multiple_of(g * width, LANES), width)

    def load(a, part):
        src = (k_hbm, v_hbm, q_hbm, g_hbm)[a]
        dst = (k_ref, v_ref, q_ref, g_ref)[a]
        cols = (slice(0, width), slice(width, heads * LANES), slice(0, heads * LANES))[part]
        return pltpu.make_async_copy(src.at[:, cols], dst.at[:, cols], load_sem.at[a, min(part, 1)])

    def each_group(body, start=0):
        def step(g, c):
            body(g)
            return c
        lax.fori_loop(start, groups, step, 0)

    greeted = greet(pair)

    load_x = pltpu.make_async_copy(x_hbm, x_ref, x_sem)
    upper = 2 * me >= n
    pl.when(upper)(load_x.start)
    for a in range(2):
        load(a, 0).start()
    pl.when(jnp.logical_not(upper))(load_x.start)
    for a in range(2):
        load(a, 1).start()

    lengths = [ll_ref[0, i] for i in range(ll_ref.shape[1])]
    starts = [jnp.int32(0)]
    for length in lengths[:-1]:
        starts.append(starts[-1] + length)

    def seg_of(pos):
        total = (starts[0] <= pos).astype(jnp.int32)
        for s in starts[1:]:
            total = total + (s <= pos).astype(jnp.int32)
        return total

    before = seg_of(first - 1)
    end = seg_of(first + B - 1)
    seg_col = seg_of(first + lax.broadcasted_iota(jnp.int32, (B, LANES), 0))
    min_ref[...] = jnp.where(seg_col == before, 1.0, 0.0).astype(F32)
    mout_ref[...] = jnp.where(seg_col == end, 1.0, 0.0).astype(F32)
    open_all = jnp.where(jnp.full((1, LANES), end) == before, 1.0, 0.0).astype(F32)
    above = lax.broadcasted_iota(jnp.int32, (LANES, LANES), 0)
    below = lax.broadcasted_iota(jnp.int32, (LANES, LANES), 1)
    tri = jnp.where(above <= below, 1.0, 0.0).astype(F32)
    carry = jnp.zeros((heads, 1), F32)
    for c in range(B // LANES):
        span = slice(c * LANES, (c + 1) * LANES)
        run = carry + lax.dot_general(
            ld_ref[:, span], tri, (((1,), (0,)), ((), ())),
            preferred_element_type=F32, precision=lax.Precision.HIGHEST,
        )
        cum_ref[:, span] = run
        carry = run[:, LANES - 1 :]

    def make_mask():
        t_pos = lax.broadcasted_iota(jnp.int32, (B, B), 0)
        u_pos = lax.broadcasted_iota(jnp.int32, (B, B), 1)
        wide = jnp.concatenate([seg_col] * (B // LANES), axis=1)
        row = seg_of(first + lax.broadcasted_iota(jnp.int32, (1, B), 1))
        same = (t_pos >= u_pos) & (wide == row)
        mask_ref[...] = jnp.where(same, 0.0, -1e30).astype(F32)

    def lanes(h):
        return pl.ds(pl.multiple_of(h * LANES, LANES), LANES)

    def weight_of(h):
        cb = colb_ref[h]
        return jnp.exp(cb[B - 1 : B, :] - cb) * mout_ref[...]

    def gamma_of(h):
        return jnp.exp(colb_ref[h]) * min_ref[...]

    def passing_of(h):
        return jnp.exp(colb_ref[h, B - 1 : B, :]) * open_all

    def decay_of(h, ts, cols):
        cb = colb_ref[h, ts, :]
        wide = jnp.concatenate([cb] * (cols // LANES), axis=1)
        row = cum_ref[pl.ds(h, 1), :cols]
        return jnp.exp((wide - row) + mask_ref[ts, :cols])

    def each_head(g, body):
        for i in range(group):
            body(g * group + i, i)

    def hop(src, dst, ss, rs, g, to):
        span = pl.ds(g * group, group)
        return pltpu.make_async_remote_copy(
            src_ref=src.at[span], dst_ref=dst.at[span], send_sem=ss.at[g], recv_sem=rs.at[g],
            device_id={"seq": to}, device_id_type=MESH,
        )

    def forward(g):
        return hop(fsend, frecv, fss, frs, g, me + 1)

    def backward(g):
        return hop(bsend, brecv, bss, brs, g, me - 1)

    def update(g):
        for part in range(2):
            @pl.when(g == part)
            def _():
                load(0, part).wait()
                load(1, part).wait()

        def column(h, i):
            colb_ref[h] = jnp.transpose(jnp.broadcast_to(cum_ref[pl.ds(h, 1), :], (LANES, B)))

        def one(h, i):
            column(h, i)
            wk = (k_ref[:, lanes(h)].astype(F32) * weight_of(h)).astype(BF16)
            upd_ref[h] = dot(wk, v_ref[:, lanes(h)], 0, 0)

        pl.when(me == n - 1)(lambda: each_head(g, column))
        pl.when(me < n - 1)(lambda: each_head(g, one))

        @pl.when(me == 0)
        def _():
            def ready(h, i):
                fsend[h] = upd_ref[h].astype(BF16)
                frecv[h] = jnp.zeros((LANES, LANES), BF16)
            each_head(g, ready)
            forward(g).start()

        @pl.when(me == n - 1)
        def _():
            def ready(h, i):
                brecv[h] = jnp.zeros((LANES, LANES), BF16)
            each_head(g, ready)

    def relay_forward(g):
        @pl.when(inside)
        def _():
            forward(g).wait_recv()

            def send(h, i):
                fsend[h] = (passing_of(h) * frecv[h].astype(F32) + upd_ref[h]).astype(BF16)
            each_head(g, send)
            forward(g).start()

    def attention(g):
        @pl.when(g == 0)
        def _():
            load(2, 2).wait()
            load(3, 2).wait()

        @pl.when(me == n - 1)
        def _():
            forward(g).wait_recv()

        def one(h, i):
            q = q_ref[:, lanes(h)]
            s = dot(q, k_ref[:, lanes(h)], 1, 1)
            s_bf = (s * decay_of(h, slice(0, B), B)).astype(BF16)
            sc_ref[h] = s_bf
            gamma = gamma_of(h)
            att = gamma * dot(q, frecv[h], 1, 0) + dot(s_bf, v_ref[:, lanes(h)], 1, 0)
            inv = lax.rsqrt(jnp.mean(att * att, axis=-1, keepdims=True) + EPS)
            normed = att * inv
            wide = g_ref[:, lanes(h)].astype(F32)
            ga = (inv * (wide - normed * jnp.mean(wide * normed, axis=-1, keepdims=True))).astype(BF16)
            ga_ref[h] = ga
            gated = (q.astype(F32) * gamma).astype(BF16)
            bs_ref[h] = dot(gated, ga, 0, 0)

        each_head(g, one)

        @pl.when(me == n - 1)
        def _():
            def ready(h, i):
                bsend[h] = bs_ref[h].astype(BF16)
            each_head(g, ready)
            backward(g).start()

    def relay_back(g):
        @pl.when(me < n - 1)
        def _():
            backward(g).wait_recv()

        @pl.when(inside)
        def _():
            def send(h, i):
                bsend[h] = (passing_of(h) * brecv[h].astype(F32) + bs_ref[h]).astype(BF16)
            each_head(g, send)
            backward(g).start()

    tile = math.gcd(B, 256)
    tiles = B // tile

    def grads(g):
        def one(h, i):
            gamma = gamma_of(h)
            w = weight_of(h)
            later = brecv[h]
            kis, vis = [None] * tiles, [None] * tiles
            for b in range(tiles):
                ts, cols = slice(b * tile, (b + 1) * tile), (b + 1) * tile
                ga = ga_ref[h, ts, :]
                q = q_ref[ts, lanes(h)]
                gs = (dot(ga, v_ref[:cols, lanes(h)], 1, 1) * decay_of(h, ts, cols)).astype(BF16)
                gq = gamma[ts] * dot(ga, frecv[h], 1, 1) + dot(gs, k_ref[:cols, lanes(h)], 1, 0)
                ki = dot(gs, q, 0, 0)
                vi = dot(sc_ref[h, ts, :cols], ga, 0, 0)
                q_ref[ts, lanes(h)] = gq.astype(BF16)
                for j in range(b + 1):
                    js = slice(j * tile, (j + 1) * tile)
                    kis[j] = ki[js] if kis[j] is None else kis[j] + ki[js]
                    vis[j] = vi[js] if vis[j] is None else vis[j] + vi[js]
            for j in range(tiles):
                js = slice(j * tile, (j + 1) * tile)
                k = k_ref[js, lanes(h)]
                gk = kis[j] + w[js] * dot(v_ref[js, lanes(h)], later, 1, 1)
                gv = vis[j] + w[js] * dot(k, later, 1, 0)
                k_ref[js, lanes(h)] = gk.astype(BF16)
                g_ref[js, lanes(h)] = gv.astype(BF16)

        each_head(g, one)
        pl.when(is_end)(lambda: ends_copy(g).start())
        gk_copy(g).start()

    def gk_copy(g):
        return pltpu.make_async_remote_copy(
            src_ref=k_ref.at[:, columns(g)], dst_ref=gm_ref.at[:, columns(g)],
            send_sem=gss.at[g], recv_sem=grs.at[g],
            device_id={"dp": mate}, device_id_type=MESH,
        )

    def ends_copy(g):
        return pltpu.make_async_remote_copy(
            src_ref=k_ref.at[:, columns(g)], dst_ref=ge_ref.at[pl.ds(0, B), columns(g)],
            send_sem=hss.at[g], recv_sem=hrs.at[g],
            device_id={"seq": hub}, device_id_type=MESH,
        )

    def pass_copy(g):
        return pltpu.make_async_remote_copy(
            src_ref=ge_ref.at[pl.ds(0, B), columns(g)], dst_ref=ge_ref.at[pl.ds(B, B), columns(g)],
            send_sem=mss.at[g], recv_sem=mrs.at[g],
            device_id={"dp": mate}, device_id_type=MESH,
        )

    def share(z, owner):
        return pl.ds(pl.multiple_of((z * 2 + owner) * rows, math.gcd(rows, LANES)), rows)

    def halves(which, base=0):
        return pl.ds(pl.multiple_of(base + which * half, math.gcd(half, LANES)), half)

    def x_copy(z):
        return pltpu.make_async_remote_copy(
            src_ref=xt_ref.at[share(z, mate)], dst_ref=xm_ref.at[z],
            send_sem=xss.at[z], recv_sem=xrs.at[z],
            device_id={"dp": mate}, device_id_type=MESH,
        )

    def turn(i, c):
        span = pl.ds(pl.multiple_of(i * LANES, LANES), LANES)
        xt_ref[span, :] = jnp.transpose(x_ref[:, span])
        return c

    def turn_inputs():
        load_x.wait()
        lax.fori_loop(0, D // LANES, turn, 0)

    def swap_inputs():
        lax.fori_loop(0, n, lambda e, c: (x_copy(far(e)).start(), c)[1], 0)

    def early_copy(e, part):
        z = far(e)
        src = (
            xt_ref.at[halves(side, (z * 2 + dp) * rows)] if part == 0 else xm_ref.at[z, halves(side)]
        )
        return pltpu.make_async_remote_copy(
            src_ref=src, dst_ref=xe_ref.at[z, halves(side), pl.ds(part * B, B)],
            send_sem=ess.at[z, part], recv_sem=ers.at[z, part],
            device_id={"seq": hub}, device_id_type=MESH,
        )

    def pair_copy(e, part, which):
        z = far(e)
        ref = xe_ref.at[z, halves(which), pl.ds(part * B, B)]
        return pltpu.make_async_remote_copy(
            src_ref=ref, dst_ref=ref, send_sem=pss.at[z, part], recv_sem=prs.at[z, part],
            device_id={"head": pair}, device_id_type=MESH,
        )

    def send_early(lo, hi):
        for j in range(lo, hi):
            if j % 2 == 1:
                x_copy(far(j // 2)).wait_recv()
            early_copy(j // 2, j % 2).start()

    def take_early(lo, hi):
        for j in range(lo, hi):
            early_copy(j // 2, j % 2).wait_recv()
            if paired:
                pair_copy(j // 2, j % 2, side).start()

    def have_early(lo, count):
        if paired:
            def one(e):
                for part in range(2):
                    pair_copy(lo + e, part, 1 - side).wait_recv()
            repeat(count, one)

    def partial(z, g):
        own = dot(xt_ref[share(z, dp), :], k_ref[:, columns(g)], 1, 0)
        return own + dot(xm_ref[z], gm_ref[:, columns(g)], 1, 0)

    def partial_extra(z, g):
        return partial(z, g) + dot(xe_ref[z], ge_ref[:, columns(g)], 1, 0)

    def term(z, g):
        down = (z < me).astype(jnp.int32)
        to = me + 1 - 2 * down
        slot = jnp.where((down == 1) & (to == z), n, z)
        return pltpu.make_async_remote_copy(
            src_ref=st_ref.at[z, g], dst_ref=st_ref.at[slot, g],
            send_sem=ss.at[z, g], recv_sem=rs.at[slot, g],
            device_id={"seq": to}, device_id_type=MESH,
        )

    def arrived(slot, g):
        pltpu.make_async_remote_copy(
            src_ref=st_ref.at[slot, g], dst_ref=st_ref.at[slot, g],
            send_sem=ss.at[0, g], recv_sem=rs.at[slot, g],
            device_id={"dp": mate}, device_id_type=MESH,
        ).wait_recv()

    def wait_x():
        @pl.when(inside)
        def _():
            lax.fori_loop(0, n, lambda z, c: (x_copy(z).wait_recv(), c)[1], 0)

        @pl.when(is_end)
        def _():
            x_copy(far(n - 1)).wait_recv()

    def take_factor(g):
        @pl.when(is_hub)
        def _():
            ends_copy(g).wait_recv()
            pass_copy(g).start()

    def send_share(e, g):
        z = far(e)
        pl.when(g == 0)(lambda: have_early(e, 1))
        st_ref[z, g] = partial_extra(z, g).astype(BF16)
        term(z, g).start()

    def send_first(g):
        gk_copy(g).wait_recv()

        @pl.when(is_hub)
        def _():
            pass_copy(g).wait_recv()
            send_share(0, g)

    def send_rest(g):
        pl.when(is_hub)(lambda: repeat(late - 1, lambda e: send_share(e + 1, g)))

    def pass_on(z, g):
        total = partial(z, g)
        arrived(z, g)
        st_ref[z, g] = (total + st_ref[z, g].astype(F32)).astype(BF16)
        term(z, g).start()

    def send_on(g):
        pl.when(is_hub)(lambda: pass_on(ext, g))
        if n > 4:
            @pl.when(jnp.logical_not(is_hub | is_end))
            def _():
                def step(j, c):
                    z = (j // 2) * (1 - j % 2) + (n - 1 - j // 2) * (j % 2)
                    pl.when(z != me)(lambda: pass_on(z, g))
                    return c
                lax.fori_loop(0, n, step, 0)

    def guarded(cond, body):
        pl.when(cond)(body)

    pieces = 2 * late
    most = pieces // 2
    pl.when(upper)(turn_inputs)
    greeted()
    for a in range(2, 4):
        load(a, 2).start()
    pl.when(upper)(swap_inputs)
    pl.when(me == n - 1)(lambda: send_early(0, most))

    ahead = min(groups, 4)

    def prepare(g):
        update(g)
        guarded(g >= ahead, lambda: relay_forward(g - ahead))

        @pl.when(inside & jnp.logical_not(upper) & (g == min(ahead, groups - 1)))
        def _():
            turn_inputs()
            swap_inputs()

    each_group(prepare)
    make_mask()

    @pl.when(me == 0)
    def _():
        turn_inputs()
        swap_inputs()
        send_early(0, pieces)

    behind = jnp.where(me == 0, groups - 1, jnp.minimum((n - 2 - me) * 3 + 2, groups - 1))
    products = groups + 1

    def iteration(i, c):
        done = i - groups
        guarded(i < ahead, lambda: relay_forward(i + groups - ahead))
        guarded(i < groups, lambda: attention(i))

        for q in range(3):
            lo, hi = pieces * q // 4, pieces * (q + 1) // 4
            at = max(0, groups - 4 + 2 * q)
            guarded(is_hub & (i == at), lambda: take_early(lo, hi))
        split = (most + pieces) // 2
        guarded((me == n - 1) & (i == 0), lambda: send_early(most, split))
        guarded((me == n - 1) & (i == 2), lambda: send_early(split, pieces))
        guarded(is_end & (done == 5), lambda: send_early(pieces, pieces + 2))
        guarded((done >= 0) & (done < groups), lambda: grads(done))
        guarded(is_hub & (done == 1), lambda: take_early(pieces * 3 // 4, pieces))

        guarded(i == products, wait_x)

        ready = i - products
        guarded((ready >= 0) & (ready < groups), lambda: take_factor(ready))
        guarded((ready >= 0) & (ready < groups), lambda: send_first(ready))
        guarded((ready >= 1) & (ready - 1 < groups), lambda: send_rest(ready - 1))
        guarded((ready >= 1) & (ready - 1 < groups), lambda: send_on(ready - 1))
        guarded(is_hub & (ready == 6), lambda: take_early(pieces, pieces + 2))
        guarded((i >= behind) & (i - behind < groups), lambda: relay_back(i - behind))
        return c

    lax.fori_loop(0, products + max(groups, 6) + 1, iteration, 0)

    def drain(g):
        @pl.when(me < n - 1)
        def _():
            forward(g).wait_send()

        @pl.when(me > 0)
        def _():
            backward(g).wait_send()

        gk_copy(g).wait_send()
        pl.when(is_end)(lambda: ends_copy(g).wait_send())
        pl.when(is_hub)(lambda: pass_copy(g).wait_send())

    each_group(drain)

    def sent_x(z, c):
        x_copy(z).wait_send()
        return c

    lax.fori_loop(0, n, sent_x, 0)

    def sent_early(e, c):
        for part in range(2):
            pl.when(is_end)(lambda: early_copy(e, part).wait_send())
            if paired:
                pl.when(is_hub)(lambda: pair_copy(e, part, side).wait_send())
        return c

    lax.fori_loop(0, n - 1, sent_early, 0)

    def settle(g):
        @pl.when(is_hub)
        def _():
            pl.when(g == 0)(lambda: have_early(late, 1))
            out_ref[:, columns(g)] = partial_extra(me, g)

        @pl.when(jnp.logical_not(is_hub))
        def _():
            out_ref[:, columns(g)] = partial(me, g)

        @pl.when(me > 1)
        def _():
            arrived(me, g)
            out_ref[:, columns(g)] += st_ref[me, g].astype(F32)

        @pl.when(me < n - 2)
        def _():
            arrived(n, g)
            out_ref[:, columns(g)] += st_ref[n, g].astype(F32)

        @pl.when(inside)
        def _():
            def step(z, c):
                pl.when(z != me)(lambda: term(z, g).wait_send())
                return c
            lax.fori_loop(0, n, step, 0)

    each_group(settle)


def layer(lengths, log_decay, x, q, k, v, g):
    heads, B = log_decay.shape
    D, F = x.shape[1], q.shape[1]
    n, group, groups, rows = sizes(heads, D)
    hbm = pl.BlockSpec(memory_space=pl.ANY)
    vmem = pl.BlockSpec(memory_space=pltpu.VMEM)
    state = (heads, LANES, LANES)
    wide = pltpu.VMEM((B, F), BF16)
    dma = pltpu.SemaphoreType.DMA
    return pl.pallas_call(
        functools.partial(layer_kernel, heads),
        out_shape=(wide, wide, pltpu.VMEM((rows, F), F32)),
        in_specs=[
            pl.BlockSpec(memory_space=pltpu.SMEM), pl.BlockSpec(memory_space=pltpu.VMEM)
        ] + [hbm] * 5,
        out_specs=(vmem, vmem, vmem),
        scratch_shapes=[pltpu.VMEM((B, F), BF16)] * 2
        + [
            pltpu.VMEM((B, D), BF16),
            pltpu.VMEM((D, B), BF16),
            pltpu.VMEM((n, rows, B), BF16),
            pltpu.VMEM((n, rows, 2 * B), BF16),
            pltpu.VMEM((B, F), BF16),
            pltpu.VMEM((2 * B, F), BF16),
            pltpu.VMEM((n + 1, groups, rows, group * LANES), BF16),
            pltpu.VMEM((heads, B), F32),
            pltpu.VMEM((heads, B, LANES), F32),
            pltpu.VMEM((B, B), F32),
            pltpu.VMEM((B, LANES), F32),
            pltpu.VMEM((B, LANES), F32),
            pltpu.VMEM(state, F32),
            pltpu.VMEM((heads, B, B), BF16),
            pltpu.VMEM((heads, B, LANES), BF16),
            pltpu.VMEM(state, F32),
        ]
        + [pltpu.VMEM(state, BF16)] * 4
        + [dma((groups,))] * 4
        + [
            dma((4, 2)), dma(()), dma((n,)), dma((n,)),
            dma((groups,)), dma((groups,)), dma((n, groups)), dma((n + 1, groups)),
        ]
        + [dma((n, 2))] * 4 + [dma((groups,))] * 4,
        compiler_params=pltpu.CompilerParams(
            collective_id=0, has_side_effects=True, vmem_limit_bytes=55 * 1024 * 1024
        ),
        name="layer",
    )(lengths, log_decay, x, q, k, v, g)


def deliver_kernel(*refs):
    count = (len(refs) - 1) // 2
    srcs, dsts, sem = refs[:count], refs[count:-1], refs[-1]
    moves = [pltpu.make_async_copy(srcs[a], dsts[a], sem.at[a]) for a in range(count)]
    for move in moves:
        move.start()
    for move in moves:
        move.wait()


def deliver(*arrays):
    hbm = pl.BlockSpec(memory_space=pl.ANY)
    vmem = pl.BlockSpec(memory_space=pltpu.VMEM)
    return pl.pallas_call(
        deliver_kernel,
        out_shape=tuple(jax.ShapeDtypeStruct(a.shape, a.dtype) for a in arrays),
        in_specs=[vmem] * len(arrays),
        out_specs=(hbm,) * len(arrays),
        scratch_shapes=[pltpu.SemaphoreType.DMA((len(arrays),))],
        compiler_params=pltpu.CompilerParams(vmem_limit_bytes=16 * 1024 * 1024),
        name="deliver",
    )(*arrays)


def body(inputs, queries, keys, values, log_decay, list_lengths, grad_out):
    gq, gv, gw = layer(
        list_lengths, log_decay[0], inputs[0], queries[0], keys[0], values[0], grad_out[0]
    )
    gq, gv, gw = deliver(gq, gv, gw)
    return gq[None], gv[None], gw


def solution(mesh):
    rows = ("groups", "dp")
    wide = P(rows, "seq", "head")
    return jax.shard_map(
        body,
        mesh=mesh,
        in_specs=(
            P(rows, "seq", None), wide, wide, wide, P(rows, "head", "seq"), P(rows, None), wide,
        ),
        out_specs=(wide, wide, P(("groups", "seq", "dp"), "head")),
        check_vma=False,
    )
```

```python
import functools
import math

import jax
import jax.numpy as jnp
from jax import lax
from jax.experimental import pallas as pl
from jax.experimental.pallas import tpu as pltpu
from jax.sharding import PartitionSpec as P

EPS = 1e-06
MESH = pl.DeviceIdType.MESH
LANES = 128
F32 = jnp.float32
BF16 = jnp.bfloat16


def dot(a, b, ca, cb):
    return lax.dot_general(a, b, (((ca,), (cb,)), ((), ())), preferred_element_type=F32)


def greet(pair):
    barrier = pltpu.get_barrier_semaphore()
    me = lax.axis_index("seq")
    n = lax.axis_size("seq")

    @pl.when(me > 0)
    def _():
        pl.semaphore_signal(barrier, inc=1, device_id={"seq": me - 1}, device_id_type=MESH)

    @pl.when(me < n - 1)
    def _():
        pl.semaphore_signal(barrier, inc=1, device_id={"seq": me + 1}, device_id_type=MESH)

    peers = (me > 0).astype(jnp.int32) + (me < n - 1).astype(jnp.int32) + 1
    mate = 1 - lax.axis_index("dp")
    pl.semaphore_signal(barrier, inc=1, device_id={"dp": mate}, device_id_type=MESH)
    if pair is not None:
        pl.semaphore_signal(barrier, inc=1, device_id={"head": pair}, device_id_type=MESH)
        peers = peers + 1
    return lambda: pl.semaphore_wait(barrier, peers)


def sizes(heads, D):
    group = math.gcd(heads, 2)
    n = lax.axis_size("seq")
    return n, group, heads // group, D // (2 * n)


def repeat(count, body):
    if count <= 3:
        for i in range(count):
            body(i)
        return

    def step(i, c):
        body(i)
        return c

    lax.fori_loop(0, count, step, 0)


def layer_kernel(
    heads, ll_ref, ld_ref, x_hbm, q_hbm, k_hbm, v_hbm, g_hbm, q_ref, g_ref, out_ref,
    k_ref, v_ref, x_ref, xt_ref, xm_ref, xe_ref, gm_ref, ge_ref, st_ref,
    cum_ref, colb_ref, mask_ref, min_ref, mout_ref, upd_ref, sc_ref, ga_ref,
    bs_ref, fsend, frecv, bsend, brecv, fss, frs, bss, brs,
    load_sem, x_sem, xss, xrs, gss, grs, ss, rs, ess, ers, pss, prs, hss, hrs, mss, mrs,
):
    me = lax.axis_index("seq")
    dp = lax.axis_index("dp")
    hx = lax.axis_index("head")
    B, D = x_ref.shape
    n, group, groups, rows = sizes(heads, D)
    first = me * B
    mate = 1 - dp
    width = group * LANES
    paired = lax.axis_size("head") % 2 == 0
    half = rows // 2 if paired else rows
    side = hx % 2 if paired else 0
    pair = hx + 1 - 2 * side if paired else None
    late = n - 2

    is_end = (me == 0) | (me == n - 1)
    is_hub = (me == 1) | (me == n - 2)
    inside = jnp.logical_not(is_end)
    low = me <= 1
    hub = jnp.where(low, 1, n - 2)
    ext = jnp.where(low, 0, n - 1)

    def far(e):
        return jnp.where(low, n - 1 - e, e)

    def columns(g):
        return pl.ds(pl.multiple_of(g * width, LANES), width)

    def load(a, part):
        src = (k_hbm, v_hbm, q_hbm, g_hbm)[a]
        dst = (k_ref, v_ref, q_ref, g_ref)[a]
        cols = (slice(0, width), slice(width, heads * LANES), slice(0, heads * LANES))[part]
        return pltpu.make_async_copy(src.at[:, cols], dst.at[:, cols], load_sem.at[a, min(part, 1)])

    def each_group(body, start=0):
        def step(g, c):
            body(g)
            return c
        lax.fori_loop(start, groups, step, 0)

    greeted = greet(pair)

    load_x = pltpu.make_async_copy(x_hbm, x_ref, x_sem)
    upper = 2 * me >= n
    pl.when(upper)(load_x.start)
    for a in range(2):
        load(a, 0).start()
    pl.when(jnp.logical_not(upper))(load_x.start)
    for a in range(2):
        load(a, 1).start()

    lengths = [ll_ref[0, i] for i in range(ll_ref.shape[1])]
    starts = [jnp.int32(0)]
    for length in lengths[:-1]:
        starts.append(starts[-1] + length)

    def seg_of(pos):
        total = (starts[0] <= pos).astype(jnp.int32)
        for s in starts[1:]:
            total = total + (s <= pos).astype(jnp.int32)
        return total

    before = seg_of(first - 1)
    end = seg_of(first + B - 1)
    seg_col = seg_of(first + lax.broadcasted_iota(jnp.int32, (B, LANES), 0))
    min_ref[...] = jnp.where(seg_col == before, 1.0, 0.0).astype(F32)
    mout_ref[...] = jnp.where(seg_col == end, 1.0, 0.0).astype(F32)
    open_all = jnp.where(jnp.full((1, LANES), end) == before, 1.0, 0.0).astype(F32)
    above = lax.broadcasted_iota(jnp.int32, (LANES, LANES), 0)
    below = lax.broadcasted_iota(jnp.int32, (LANES, LANES), 1)
    tri = jnp.where(above <= below, 1.0, 0.0).astype(F32)
    carry = jnp.zeros((heads, 1), F32)
    for c in range(B // LANES):
        span = slice(c * LANES, (c + 1) * LANES)
        run = carry + lax.dot_general(
            ld_ref[:, span], tri, (((1,), (0,)), ((), ())),
            preferred_element_type=F32, precision=lax.Precision.HIGHEST,
        )
        cum_ref[:, span] = run
        carry = run[:, LANES - 1 :]

    def make_mask():
        t_pos = lax.broadcasted_iota(jnp.int32, (B, B), 0)
        u_pos = lax.broadcasted_iota(jnp.int32, (B, B), 1)
        wide = jnp.concatenate([seg_col] * (B // LANES), axis=1)
        row = seg_of(first + lax.broadcasted_iota(jnp.int32, (1, B), 1))
        same = (t_pos >= u_pos) & (wide == row)
        mask_ref[...] = jnp.where(same, 0.0, -1e30).astype(F32)

    def lanes(h):
        return pl.ds(pl.multiple_of(h * LANES, LANES), LANES)

    def weight_of(h):
        cb = colb_ref[h]
        return jnp.exp(cb[B - 1 : B, :] - cb) * mout_ref[...]

    def gamma_of(h):
        return jnp.exp(colb_ref[h]) * min_ref[...]

    def passing_of(h):
        return jnp.exp(colb_ref[h, B - 1 : B, :]) * open_all

    def decay_of(h, ts, cols):
        cb = colb_ref[h, ts, :]
        wide = jnp.concatenate([cb] * (cols // LANES), axis=1)
        row = cum_ref[pl.ds(h, 1), :cols]
        return jnp.exp((wide - row) + mask_ref[ts, :cols])

    def each_head(g, body):
        for i in range(group):
            body(g * group + i, i)

    def hop(src, dst, ss, rs, g, to):
        span = pl.ds(g * group, group)
        return pltpu.make_async_remote_copy(
            src_ref=src.at[span], dst_ref=dst.at[span], send_sem=ss.at[g], recv_sem=rs.at[g],
            device_id={"seq": to}, device_id_type=MESH,
        )

    def forward(g):
        return hop(fsend, frecv, fss, frs, g, me + 1)

    def backward(g):
        return hop(bsend, brecv, bss, brs, g, me - 1)

    def update(g):
        for part in range(2):
            @pl.when(g == part)
            def _():
                load(0, part).wait()
                load(1, part).wait()

        def column(h, i):
            colb_ref[h] = jnp.transpose(jnp.broadcast_to(cum_ref[pl.ds(h, 1), :], (LANES, B)))

        def one(h, i):
            column(h, i)
            wk = (k_ref[:, lanes(h)].astype(F32) * weight_of(h)).astype(BF16)
            upd_ref[h] = dot(wk, v_ref[:, lanes(h)], 0, 0)

        pl.when(me == n - 1)(lambda: each_head(g, column))
        pl.when(me < n - 1)(lambda: each_head(g, one))

        @pl.when(me == 0)
        def _():
            def ready(h, i):
                fsend[h] = upd_ref[h].astype(BF16)
                frecv[h] = jnp.zeros((LANES, LANES), BF16)
            each_head(g, ready)
            forward(g).start()

        @pl.when(me == n - 1)
        def _():
            def ready(h, i):
                brecv[h] = jnp.zeros((LANES, LANES), BF16)
            each_head(g, ready)

    def relay_forward(g):
        @pl.when(inside)
        def _():
            forward(g).wait_recv()

            def send(h, i):
                fsend[h] = (passing_of(h) * frecv[h].astype(F32) + upd_ref[h]).astype(BF16)
            each_head(g, send)
            forward(g).start()

    def attention(g):
        @pl.when(g == 0)
        def _():
            load(2, 2).wait()
            load(3, 2).wait()

        @pl.when(me == n - 1)
        def _():
            forward(g).wait_recv()

        def one(h, i):
            q = q_ref[:, lanes(h)]
            s = dot(q, k_ref[:, lanes(h)], 1, 1)
            s_bf = (s * decay_of(h, slice(0, B), B)).astype(BF16)
            sc_ref[h] = s_bf
            gamma = gamma_of(h)
            att = gamma * dot(q, frecv[h], 1, 0) + dot(s_bf, v_ref[:, lanes(h)], 1, 0)
            inv = lax.rsqrt(jnp.mean(att * att, axis=-1, keepdims=True) + EPS)
            normed = att * inv
            wide = g_ref[:, lanes(h)].astype(F32)
            ga = (inv * (wide - normed * jnp.mean(wide * normed, axis=-1, keepdims=True))).astype(BF16)
            ga_ref[h] = ga
            gated = (q.astype(F32) * gamma).astype(BF16)
            bs_ref[h] = dot(gated, ga, 0, 0)

        each_head(g, one)

        @pl.when(me == n - 1)
        def _():
            def ready(h, i):
                bsend[h] = bs_ref[h].astype(BF16)
            each_head(g, ready)
            backward(g).start()

    def relay_back(g):
        @pl.when(me < n - 1)
        def _():
            backward(g).wait_recv()

        @pl.when(inside)
        def _():
            def send(h, i):
                bsend[h] = (passing_of(h) * brecv[h].astype(F32) + bs_ref[h]).astype(BF16)
            each_head(g, send)
            backward(g).start()

    tile = math.gcd(B, 256)
    tiles = B // tile

    def grads(g):
        def one(h, i):
            gamma = gamma_of(h)
            w = weight_of(h)
            later = brecv[h]
            kis, vis = [None] * tiles, [None] * tiles
            for b in range(tiles):
                ts, cols = slice(b * tile, (b + 1) * tile), (b + 1) * tile
                ga = ga_ref[h, ts, :]
                q = q_ref[ts, lanes(h)]
                gs = (dot(ga, v_ref[:cols, lanes(h)], 1, 1) * decay_of(h, ts, cols)).astype(BF16)
                gq = gamma[ts] * dot(ga, frecv[h], 1, 1) + dot(gs, k_ref[:cols, lanes(h)], 1, 0)
                ki = dot(gs, q, 0, 0)
                vi = dot(sc_ref[h, ts, :cols], ga, 0, 0)
                q_ref[ts, lanes(h)] = gq.astype(BF16)
                for j in range(b + 1):
                    js = slice(j * tile, (j + 1) * tile)
                    kis[j] = ki[js] if kis[j] is None else kis[j] + ki[js]
                    vis[j] = vi[js] if vis[j] is None else vis[j] + vi[js]
            for j in range(tiles):
                js = slice(j * tile, (j + 1) * tile)
                k = k_ref[js, lanes(h)]
                gk = kis[j] + w[js] * dot(v_ref[js, lanes(h)], later, 1, 1)
                gv = vis[j] + w[js] * dot(k, later, 1, 0)
                k_ref[js, lanes(h)] = gk.astype(BF16)
                g_ref[js, lanes(h)] = gv.astype(BF16)

        each_head(g, one)
        pl.when(is_end)(lambda: ends_copy(g).start())
        gk_copy(g).start()

    def gk_copy(g):
        return pltpu.make_async_remote_copy(
            src_ref=k_ref.at[:, columns(g)], dst_ref=gm_ref.at[:, columns(g)],
            send_sem=gss.at[g], recv_sem=grs.at[g],
            device_id={"dp": mate}, device_id_type=MESH,
        )

    def ends_copy(g):
        return pltpu.make_async_remote_copy(
            src_ref=k_ref.at[:, columns(g)], dst_ref=ge_ref.at[pl.ds(0, B), columns(g)],
            send_sem=hss.at[g], recv_sem=hrs.at[g],
            device_id={"seq": hub}, device_id_type=MESH,
        )

    def pass_copy(g):
        return pltpu.make_async_remote_copy(
            src_ref=ge_ref.at[pl.ds(0, B), columns(g)], dst_ref=ge_ref.at[pl.ds(B, B), columns(g)],
            send_sem=mss.at[g], recv_sem=mrs.at[g],
            device_id={"dp": mate}, device_id_type=MESH,
        )

    def share(z, owner):
        return pl.ds(pl.multiple_of((z * 2 + owner) * rows, math.gcd(rows, LANES)), rows)

    def halves(which, base=0):
        return pl.ds(pl.multiple_of(base + which * half, math.gcd(half, LANES)), half)

    def x_copy(z):
        return pltpu.make_async_remote_copy(
            src_ref=xt_ref.at[share(z, mate)], dst_ref=xm_ref.at[z],
            send_sem=xss.at[z], recv_sem=xrs.at[z],
            device_id={"dp": mate}, device_id_type=MESH,
        )

    def turn(i, c):
        span = pl.ds(pl.multiple_of(i * LANES, LANES), LANES)
        xt_ref[span, :] = jnp.transpose(x_ref[:, span])
        return c

    def turn_inputs():
        load_x.wait()
        lax.fori_loop(0, D // LANES, turn, 0)

    def swap_inputs():
        lax.fori_loop(0, n, lambda e, c: (x_copy(far(e)).start(), c)[1], 0)

    def early_copy(e, part):
        z = far(e)
        src = (
            xt_ref.at[halves(side, (z * 2 + dp) * rows)] if part == 0 else xm_ref.at[z, halves(side)]
        )
        return pltpu.make_async_remote_copy(
            src_ref=src, dst_ref=xe_ref.at[z, halves(side), pl.ds(part * B, B)],
            send_sem=ess.at[z, part], recv_sem=ers.at[z, part],
            device_id={"seq": hub}, device_id_type=MESH,
        )

    def pair_copy(e, part, which):
        z = far(e)
        ref = xe_ref.at[z, halves(which), pl.ds(part * B, B)]
        return pltpu.make_async_remote_copy(
            src_ref=ref, dst_ref=ref, send_sem=pss.at[z, part], recv_sem=prs.at[z, part],
            device_id={"head": pair}, device_id_type=MESH,
        )

    def send_early(lo, hi):
        for j in range(lo, hi):
            if j % 2 == 1:
                x_copy(far(j // 2)).wait_recv()
            early_copy(j // 2, j % 2).start()

    def take_early(lo, hi):
        for j in range(lo, hi):
            early_copy(j // 2, j % 2).wait_recv()
            if paired:
                pair_copy(j // 2, j % 2, side).start()

    def have_early(lo, count):
        if paired:
            def one(e):
                for part in range(2):
                    pair_copy(lo + e, part, 1 - side).wait_recv()
            repeat(count, one)

    def partial(z, g):
        own = dot(xt_ref[share(z, dp), :], k_ref[:, columns(g)], 1, 0)
        return own + dot(xm_ref[z], gm_ref[:, columns(g)], 1, 0)

    def partial_extra(z, g):
        return partial(z, g) + dot(xe_ref[z], ge_ref[:, columns(g)], 1, 0)

    def term(z, g):
        down = (z < me).astype(jnp.int32)
        to = me + 1 - 2 * down
        slot = jnp.where((down == 1) & (to == z), n, z)
        return pltpu.make_async_remote_copy(
            src_ref=st_ref.at[z, g], dst_ref=st_ref.at[slot, g],
            send_sem=ss.at[z, g], recv_sem=rs.at[slot, g],
            device_id={"seq": to}, device_id_type=MESH,
        )

    def arrived(slot, g):
        pltpu.make_async_remote_copy(
            src_ref=st_ref.at[slot, g], dst_ref=st_ref.at[slot, g],
            send_sem=ss.at[0, g], recv_sem=rs.at[slot, g],
            device_id={"dp": mate}, device_id_type=MESH,
        ).wait_recv()

    def wait_x():
        @pl.when(inside)
        def _():
            lax.fori_loop(0, n, lambda z, c: (x_copy(z).wait_recv(), c)[1], 0)

        @pl.when(is_end)
        def _():
            x_copy(far(n - 1)).wait_recv()

    def take_factor(g):
        @pl.when(is_hub)
        def _():
            ends_copy(g).wait_recv()
            pass_copy(g).start()

    def send_share(e, g):
        z = far(e)
        pl.when(g == 0)(lambda: have_early(e, 1))
        st_ref[z, g] = partial_extra(z, g).astype(BF16)
        term(z, g).start()

    def send_first(g):
        gk_copy(g).wait_recv()

        @pl.when(is_hub)
        def _():
            pass_copy(g).wait_recv()
            send_share(0, g)

    def send_rest(g):
        pl.when(is_hub)(lambda: repeat(late - 1, lambda e: send_share(e + 1, g)))

    def pass_on(z, g):
        total = partial(z, g)
        arrived(z, g)
        st_ref[z, g] = (total + st_ref[z, g].astype(F32)).astype(BF16)
        term(z, g).start()

    def send_on(g):
        pl.when(is_hub)(lambda: pass_on(ext, g))
        if n > 4:
            @pl.when(jnp.logical_not(is_hub | is_end))
            def _():
                def step(j, c):
                    z = (j // 2) * (1 - j % 2) + (n - 1 - j // 2) * (j % 2)
                    pl.when(z != me)(lambda: pass_on(z, g))
                    return c
                lax.fori_loop(0, n, step, 0)

    def guarded(cond, body):
        pl.when(cond)(body)

    pieces = 2 * late
    most = pieces * 3 // 4
    pl.when(upper & inside)(turn_inputs)
    greeted()
    for a in range(2, 4):
        load(a, 2).start()
    pl.when(upper & inside)(swap_inputs)

    @pl.when(me == n - 1)
    def _():
        if 2 * rows % LANES == 0:
            spans = 2 * rows // LANES

            def share_turn(e):
                z = far(e)
                lax.fori_loop(z * spans, (z + 1) * spans, turn, 0)
                x_copy(z).start()

            load_x.wait()
            share_turn(0)
            send_early(0, 1)
            lax.fori_loop(1, n, lambda e, c: (share_turn(e), c)[1], 0)
        else:
            turn_inputs()
            swap_inputs()
            send_early(0, 1)
        send_early(1, most)

    ahead = min(groups, 4)

    def prepare(g):
        update(g)
        guarded(g >= ahead, lambda: relay_forward(g - ahead))

        @pl.when(inside & jnp.logical_not(upper) & (g == min(ahead, groups - 1)))
        def _():
            turn_inputs()
            swap_inputs()

    each_group(prepare)
    make_mask()

    @pl.when(me == 0)
    def _():
        turn_inputs()
        swap_inputs()
        send_early(0, pieces)

    behind = jnp.where(me == 0, groups - 1, jnp.minimum((n - 2 - me) * 3 + 1, groups - 1))
    products = groups + 1

    def iteration(i, c):
        done = i - groups
        guarded(i < ahead, lambda: relay_forward(i + groups - ahead))
        guarded(i < groups, lambda: attention(i))

        for q in range(3):
            lo, hi = pieces * q // 4, pieces * (q + 1) // 4
            at = max(0, groups - 4 + 2 * q)
            guarded(is_hub & (i == at), lambda: take_early(lo, hi))
        guarded((me == n - 1) & (i == 1), lambda: send_early(most, pieces))
        guarded(is_end & (done == 5), lambda: send_early(pieces, pieces + 2))
        guarded((done >= 0) & (done < groups), lambda: grads(done))
        guarded(is_hub & (done == 1), lambda: take_early(pieces * 3 // 4, pieces))

        guarded(i == products, wait_x)

        ready = i - products
        guarded((ready >= 1) & (ready <= groups // 2), lambda: send_rest(ready - 1))
        guarded((ready >= 0) & (ready < groups), lambda: take_factor(ready))
        guarded((ready >= 0) & (ready < groups), lambda: send_first(ready))
        guarded((ready > groups // 2) & (ready - 1 < groups), lambda: send_rest(ready - 1))
        guarded((ready >= 1) & (ready - 1 < groups), lambda: send_on(ready - 1))
        guarded(is_hub & (ready == 6), lambda: take_early(pieces, pieces + 2))
        guarded((i >= behind) & (i - behind < groups), lambda: relay_back(i - behind))
        return c

    lax.fori_loop(0, products + max(groups, 6) + 1, iteration, 0)

    def drain(g):
        @pl.when(me < n - 1)
        def _():
            forward(g).wait_send()

        @pl.when(me > 0)
        def _():
            backward(g).wait_send()

        gk_copy(g).wait_send()
        pl.when(is_end)(lambda: ends_copy(g).wait_send())
        pl.when(is_hub)(lambda: pass_copy(g).wait_send())

    each_group(drain)

    def sent_x(z, c):
        x_copy(z).wait_send()
        return c

    lax.fori_loop(0, n, sent_x, 0)

    def sent_early(e, c):
        for part in range(2):
            pl.when(is_end)(lambda: early_copy(e, part).wait_send())
            if paired:
                pl.when(is_hub)(lambda: pair_copy(e, part, side).wait_send())
        return c

    lax.fori_loop(0, n - 1, sent_early, 0)

    def settle(g):
        @pl.when(is_hub)
        def _():
            pl.when(g == 0)(lambda: have_early(late, 1))
            out_ref[:, columns(g)] = partial_extra(me, g)

        @pl.when(jnp.logical_not(is_hub))
        def _():
            out_ref[:, columns(g)] = partial(me, g)

        @pl.when(me > 1)
        def _():
            arrived(me, g)
            out_ref[:, columns(g)] += st_ref[me, g].astype(F32)

        @pl.when(me < n - 2)
        def _():
            arrived(n, g)
            out_ref[:, columns(g)] += st_ref[n, g].astype(F32)

        @pl.when(inside)
        def _():
            def step(z, c):
                pl.when(z != me)(lambda: term(z, g).wait_send())
                return c
            lax.fori_loop(0, n, step, 0)

    each_group(settle)


def layer(lengths, log_decay, x, q, k, v, g):
    heads, B = log_decay.shape
    D, F = x.shape[1], q.shape[1]
    n, group, groups, rows = sizes(heads, D)
    hbm = pl.BlockSpec(memory_space=pl.ANY)
    vmem = pl.BlockSpec(memory_space=pltpu.VMEM)
    state = (heads, LANES, LANES)
    wide = pltpu.VMEM((B, F), BF16)
    dma = pltpu.SemaphoreType.DMA
    return pl.pallas_call(
        functools.partial(layer_kernel, heads),
        out_shape=(wide, wide, pltpu.VMEM((rows, F), F32)),
        in_specs=[
            pl.BlockSpec(memory_space=pltpu.SMEM), pl.BlockSpec(memory_space=pltpu.VMEM)
        ] + [hbm] * 5,
        out_specs=(vmem, vmem, vmem),
        scratch_shapes=[pltpu.VMEM((B, F), BF16)] * 2
        + [
            pltpu.VMEM((B, D), BF16),
            pltpu.VMEM((D, B), BF16),
            pltpu.VMEM((n, rows, B), BF16),
            pltpu.VMEM((n, rows, 2 * B), BF16),
            pltpu.VMEM((B, F), BF16),
            pltpu.VMEM((2 * B, F), BF16),
            pltpu.VMEM((n + 1, groups, rows, group * LANES), BF16),
            pltpu.VMEM((heads, B), F32),
            pltpu.VMEM((heads, B, LANES), F32),
            pltpu.VMEM((B, B), F32),
            pltpu.VMEM((B, LANES), F32),
            pltpu.VMEM((B, LANES), F32),
            pltpu.VMEM(state, F32),
            pltpu.VMEM((heads, B, B), BF16),
            pltpu.VMEM((heads, B, LANES), BF16),
            pltpu.VMEM(state, F32),
        ]
        + [pltpu.VMEM(state, BF16)] * 4
        + [dma((groups,))] * 4
        + [
            dma((4, 2)), dma(()), dma((n,)), dma((n,)),
            dma((groups,)), dma((groups,)), dma((n, groups)), dma((n + 1, groups)),
        ]
        + [dma((n, 2))] * 4 + [dma((groups,))] * 4,
        compiler_params=pltpu.CompilerParams(
            collective_id=0, has_side_effects=True, vmem_limit_bytes=55 * 1024 * 1024
        ),
        name="layer",
    )(lengths, log_decay, x, q, k, v, g)


def deliver_kernel(*refs):
    count = (len(refs) - 1) // 2
    srcs, dsts, sem = refs[:count], refs[count:-1], refs[-1]
    moves = [pltpu.make_async_copy(srcs[a], dsts[a], sem.at[a]) for a in range(count)]
    for move in moves:
        move.start()
    for move in moves:
        move.wait()


def deliver(*arrays):
    hbm = pl.BlockSpec(memory_space=pl.ANY)
    vmem = pl.BlockSpec(memory_space=pltpu.VMEM)
    return pl.pallas_call(
        deliver_kernel,
        out_shape=tuple(jax.ShapeDtypeStruct(a.shape, a.dtype) for a in arrays),
        in_specs=[vmem] * len(arrays),
        out_specs=(hbm,) * len(arrays),
        scratch_shapes=[pltpu.SemaphoreType.DMA((len(arrays),))],
        compiler_params=pltpu.CompilerParams(vmem_limit_bytes=16 * 1024 * 1024),
        name="deliver",
    )(*arrays)


def body(inputs, queries, keys, values, log_decay, list_lengths, grad_out):
    gq, gv, gw = layer(
        list_lengths, log_decay[0], inputs[0], queries[0], keys[0], values[0], grad_out[0]
    )
    gq, gv, gw = deliver(gq, gv, gw)
    return gq[None], gv[None], gw


def solution(mesh):
    rows = ("groups", "dp")
    wide = P(rows, "seq", "head")
    return jax.shard_map(
        body,
        mesh=mesh,
        in_specs=(
            P(rows, "seq", None), wide, wide, wide, P(rows, "head", "seq"), P(rows, None), wide,
        ),
        out_specs=(wide, wide, P(("groups", "seq", "dp"), "head")),
        check_vma=False,
    )
```

```python
import functools
import math

import jax
import jax.numpy as jnp
from jax import lax
from jax.experimental import pallas as pl
from jax.experimental.pallas import tpu as pltpu
from jax.sharding import PartitionSpec as P

EPS = 1e-06
MESH = pl.DeviceIdType.MESH
LANES = 128
F32 = jnp.float32
BF16 = jnp.bfloat16


def dot(a, b, ca, cb):
    return lax.dot_general(a, b, (((ca,), (cb,)), ((), ())), preferred_element_type=F32)


def greet(pair):
    barrier = pltpu.get_barrier_semaphore()
    me = lax.axis_index("seq")
    n = lax.axis_size("seq")

    @pl.when(me > 0)
    def _():
        pl.semaphore_signal(barrier, inc=1, device_id={"seq": me - 1}, device_id_type=MESH)

    @pl.when(me < n - 1)
    def _():
        pl.semaphore_signal(barrier, inc=1, device_id={"seq": me + 1}, device_id_type=MESH)

    peers = (me > 0).astype(jnp.int32) + (me < n - 1).astype(jnp.int32) + 1
    mate = 1 - lax.axis_index("dp")
    pl.semaphore_signal(barrier, inc=1, device_id={"dp": mate}, device_id_type=MESH)
    if pair is not None:
        pl.semaphore_signal(barrier, inc=1, device_id={"head": pair}, device_id_type=MESH)
        peers = peers + 1
    return lambda: pl.semaphore_wait(barrier, peers)


def sizes(heads, D):
    group = math.gcd(heads, 2)
    n = lax.axis_size("seq")
    return n, group, heads // group, D // (2 * n)


def repeat(count, body):
    if count <= 3:
        for i in range(count):
            body(i)
        return

    def step(i, c):
        body(i)
        return c

    lax.fori_loop(0, count, step, 0)


def layer_kernel(
    heads, ll_ref, ld_ref, x_hbm, q_hbm, k_hbm, v_hbm, g_hbm, q_ref, g_ref, out_ref,
    k_ref, v_ref, x_ref, xt_ref, xm_ref, xe_ref, gm_ref, ge_ref, st_ref,
    cum_ref, colb_ref, mask_ref, min_ref, mout_ref, upd_ref, sc_ref, ga_ref,
    bs_ref, fsend, frecv, bsend, brecv, fss, frs, bss, brs,
    load_sem, x_sem, xss, xrs, gss, grs, ss, rs, ess, ers, pss, prs, hss, hrs, mss, mrs,
):
    me = lax.axis_index("seq")
    dp = lax.axis_index("dp")
    hx = lax.axis_index("head")
    B, D = x_ref.shape
    n, group, groups, rows = sizes(heads, D)
    first = me * B
    mate = 1 - dp
    width = group * LANES
    paired = lax.axis_size("head") % 2 == 0
    half = rows // 2 if paired else rows
    side = hx % 2 if paired else 0
    pair = hx + 1 - 2 * side if paired else None
    late = n - 2

    is_end = (me == 0) | (me == n - 1)
    is_hub = (me == 1) | (me == n - 2)
    inside = jnp.logical_not(is_end)
    low = me <= 1
    hub = jnp.where(low, 1, n - 2)
    ext = jnp.where(low, 0, n - 1)

    def far(e):
        return jnp.where(low, n - 1 - e, e)

    def columns(g):
        return pl.ds(pl.multiple_of(g * width, LANES), width)

    def load(a, part):
        src = (k_hbm, v_hbm, q_hbm, g_hbm)[a]
        dst = (k_ref, v_ref, q_ref, g_ref)[a]
        cols = (slice(0, width), slice(width, heads * LANES), slice(0, heads * LANES))[part]
        return pltpu.make_async_copy(src.at[:, cols], dst.at[:, cols], load_sem.at[a, min(part, 1)])

    def each_group(body, start=0):
        def step(g, c):
            body(g)
            return c
        lax.fori_loop(start, groups, step, 0)

    greeted = greet(pair)

    load_x = pltpu.make_async_copy(x_hbm, x_ref, x_sem)
    upper = 2 * me >= n
    pl.when(upper)(load_x.start)
    for a in range(2):
        load(a, 0).start()
    pl.when(jnp.logical_not(upper))(load_x.start)
    for a in range(2):
        load(a, 1).start()

    lengths = [ll_ref[0, i] for i in range(ll_ref.shape[1])]
    starts = [jnp.int32(0)]
    for length in lengths[:-1]:
        starts.append(starts[-1] + length)

    def seg_of(pos):
        total = (starts[0] <= pos).astype(jnp.int32)
        for s in starts[1:]:
            total = total + (s <= pos).astype(jnp.int32)
        return total

    before = seg_of(first - 1)
    end = seg_of(first + B - 1)
    seg_col = seg_of(first + lax.broadcasted_iota(jnp.int32, (B, LANES), 0))
    min_ref[...] = jnp.where(seg_col == before, 1.0, 0.0).astype(F32)
    mout_ref[...] = jnp.where(seg_col == end, 1.0, 0.0).astype(F32)
    open_all = jnp.where(jnp.full((1, LANES), end) == before, 1.0, 0.0).astype(F32)
    above = lax.broadcasted_iota(jnp.int32, (LANES, LANES), 0)
    below = lax.broadcasted_iota(jnp.int32, (LANES, LANES), 1)
    tri = jnp.where(above <= below, 1.0, 0.0).astype(F32)
    carry = jnp.zeros((heads, 1), F32)
    for c in range(B // LANES):
        span = slice(c * LANES, (c + 1) * LANES)
        run = carry + lax.dot_general(
            ld_ref[:, span], tri, (((1,), (0,)), ((), ())),
            preferred_element_type=F32, precision=lax.Precision.HIGHEST,
        )
        cum_ref[:, span] = run
        carry = run[:, LANES - 1 :]

    def make_mask():
        t_pos = lax.broadcasted_iota(jnp.int32, (B, B), 0)
        u_pos = lax.broadcasted_iota(jnp.int32, (B, B), 1)
        wide = jnp.concatenate([seg_col] * (B // LANES), axis=1)
        row = seg_of(first + lax.broadcasted_iota(jnp.int32, (1, B), 1))
        same = (t_pos >= u_pos) & (wide == row)
        mask_ref[...] = jnp.where(same, 0.0, -1e30).astype(F32)

    def lanes(h):
        return pl.ds(pl.multiple_of(h * LANES, LANES), LANES)

    def weight_of(h):
        cb = colb_ref[h]
        return jnp.exp(cb[B - 1 : B, :] - cb) * mout_ref[...]

    def gamma_of(h):
        return jnp.exp(colb_ref[h]) * min_ref[...]

    def passing_of(h):
        return jnp.exp(colb_ref[h, B - 1 : B, :]) * open_all

    def decay_of(h, ts, cols):
        cb = colb_ref[h, ts, :]
        wide = jnp.concatenate([cb] * (cols // LANES), axis=1)
        row = cum_ref[pl.ds(h, 1), :cols]
        return jnp.exp((wide - row) + mask_ref[ts, :cols])

    def each_head(g, body):
        for i in range(group):
            body(g * group + i, i)

    def hop(src, dst, ss, rs, g, to):
        span = pl.ds(g * group, group)
        return pltpu.make_async_remote_copy(
            src_ref=src.at[span], dst_ref=dst.at[span], send_sem=ss.at[g], recv_sem=rs.at[g],
            device_id={"seq": to}, device_id_type=MESH,
        )

    def forward(g):
        return hop(fsend, frecv, fss, frs, g, me + 1)

    def backward(g):
        return hop(bsend, brecv, bss, brs, g, me - 1)

    def update(g):
        for part in range(2):
            @pl.when(g == part)
            def _():
                load(0, part).wait()
                load(1, part).wait()

        def column(h, i):
            colb_ref[h] = jnp.transpose(jnp.broadcast_to(cum_ref[pl.ds(h, 1), :], (LANES, B)))

        def one(h, i):
            column(h, i)
            wk = (k_ref[:, lanes(h)].astype(F32) * weight_of(h)).astype(BF16)
            upd_ref[h] = dot(wk, v_ref[:, lanes(h)], 0, 0)

        pl.when(me == n - 1)(lambda: each_head(g, column))
        pl.when(me < n - 1)(lambda: each_head(g, one))

        @pl.when(me == 0)
        def _():
            def ready(h, i):
                fsend[h] = upd_ref[h].astype(BF16)
                frecv[h] = jnp.zeros((LANES, LANES), BF16)
            each_head(g, ready)
            forward(g).start()

        @pl.when(me == n - 1)
        def _():
            def ready(h, i):
                brecv[h] = jnp.zeros((LANES, LANES), BF16)
            each_head(g, ready)

    def relay_forward(g):
        @pl.when(inside)
        def _():
            forward(g).wait_recv()

            def send(h, i):
                fsend[h] = (passing_of(h) * frecv[h].astype(F32) + upd_ref[h]).astype(BF16)
            each_head(g, send)
            forward(g).start()

    def attention(g):
        @pl.when(g == 0)
        def _():
            load(2, 2).wait()
            load(3, 2).wait()

        @pl.when(me == n - 1)
        def _():
            forward(g).wait_recv()

        def one(h, i):
            q = q_ref[:, lanes(h)]
            s = dot(q, k_ref[:, lanes(h)], 1, 1)
            s_bf = (s * decay_of(h, slice(0, B), B)).astype(BF16)
            sc_ref[h] = s_bf
            gamma = gamma_of(h)
            att = gamma * dot(q, frecv[h], 1, 0) + dot(s_bf, v_ref[:, lanes(h)], 1, 0)
            inv = lax.rsqrt(jnp.mean(att * att, axis=-1, keepdims=True) + EPS)
            normed = att * inv
            wide = g_ref[:, lanes(h)].astype(F32)
            ga = (inv * (wide - normed * jnp.mean(wide * normed, axis=-1, keepdims=True))).astype(BF16)
            ga_ref[h] = ga
            gated = (q.astype(F32) * gamma).astype(BF16)
            bs_ref[h] = dot(gated, ga, 0, 0)

        each_head(g, one)

        @pl.when(me == n - 1)
        def _():
            def ready(h, i):
                bsend[h] = bs_ref[h].astype(BF16)
            each_head(g, ready)
            backward(g).start()

    def relay_back(g):
        @pl.when(me < n - 1)
        def _():
            backward(g).wait_recv()

        @pl.when(inside)
        def _():
            def send(h, i):
                bsend[h] = (passing_of(h) * brecv[h].astype(F32) + bs_ref[h]).astype(BF16)
            each_head(g, send)
            backward(g).start()

    tile = math.gcd(B, 256)
    tiles = B // tile

    def grads(g):
        def one(h, i):
            gamma = gamma_of(h)
            w = weight_of(h)
            later = brecv[h]
            kis, vis = [None] * tiles, [None] * tiles
            for b in range(tiles):
                ts, cols = slice(b * tile, (b + 1) * tile), (b + 1) * tile
                ga = ga_ref[h, ts, :]
                q = q_ref[ts, lanes(h)]
                gs = (dot(ga, v_ref[:cols, lanes(h)], 1, 1) * decay_of(h, ts, cols)).astype(BF16)
                gq = gamma[ts] * dot(ga, frecv[h], 1, 1) + dot(gs, k_ref[:cols, lanes(h)], 1, 0)
                ki = dot(gs, q, 0, 0)
                vi = dot(sc_ref[h, ts, :cols], ga, 0, 0)
                q_ref[ts, lanes(h)] = gq.astype(BF16)
                for j in range(b + 1):
                    js = slice(j * tile, (j + 1) * tile)
                    kis[j] = ki[js] if kis[j] is None else kis[j] + ki[js]
                    vis[j] = vi[js] if vis[j] is None else vis[j] + vi[js]
            for j in range(tiles):
                js = slice(j * tile, (j + 1) * tile)
                k = k_ref[js, lanes(h)]
                gk = kis[j] + w[js] * dot(v_ref[js, lanes(h)], later, 1, 1)
                gv = vis[j] + w[js] * dot(k, later, 1, 0)
                k_ref[js, lanes(h)] = gk.astype(BF16)
                g_ref[js, lanes(h)] = gv.astype(BF16)

        each_head(g, one)
        pl.when(is_end)(lambda: ends_copy(g).start())
        gk_copy(g).start()

    def gk_copy(g):
        return pltpu.make_async_remote_copy(
            src_ref=k_ref.at[:, columns(g)], dst_ref=gm_ref.at[:, columns(g)],
            send_sem=gss.at[g], recv_sem=grs.at[g],
            device_id={"dp": mate}, device_id_type=MESH,
        )

    def ends_copy(g):
        return pltpu.make_async_remote_copy(
            src_ref=k_ref.at[:, columns(g)], dst_ref=ge_ref.at[pl.ds(0, B), columns(g)],
            send_sem=hss.at[g], recv_sem=hrs.at[g],
            device_id={"seq": hub}, device_id_type=MESH,
        )

    def pass_copy(g):
        return pltpu.make_async_remote_copy(
            src_ref=ge_ref.at[pl.ds(0, B), columns(g)], dst_ref=ge_ref.at[pl.ds(B, B), columns(g)],
            send_sem=mss.at[g], recv_sem=mrs.at[g],
            device_id={"dp": mate}, device_id_type=MESH,
        )

    def share(z, owner):
        return pl.ds(pl.multiple_of((z * 2 + owner) * rows, math.gcd(rows, LANES)), rows)

    def halves(which, base=0):
        return pl.ds(pl.multiple_of(base + which * half, math.gcd(half, LANES)), half)

    def x_copy(z):
        return pltpu.make_async_remote_copy(
            src_ref=xt_ref.at[share(z, mate)], dst_ref=xm_ref.at[z],
            send_sem=xss.at[z], recv_sem=xrs.at[z],
            device_id={"dp": mate}, device_id_type=MESH,
        )

    def turn(i, c):
        span = pl.ds(pl.multiple_of(i * LANES, LANES), LANES)
        xt_ref[span, :] = jnp.transpose(x_ref[:, span])
        return c

    def turn_inputs():
        load_x.wait()
        lax.fori_loop(0, D // LANES, turn, 0)

    def swap_inputs():
        lax.fori_loop(0, n, lambda e, c: (x_copy(far(e)).start(), c)[1], 0)

    def early_copy(e, part):
        z = far(e)
        src = (
            xt_ref.at[halves(side, (z * 2 + dp) * rows)] if part == 0 else xm_ref.at[z, halves(side)]
        )
        return pltpu.make_async_remote_copy(
            src_ref=src, dst_ref=xe_ref.at[z, halves(side), pl.ds(part * B, B)],
            send_sem=ess.at[z, part], recv_sem=ers.at[z, part],
            device_id={"seq": hub}, device_id_type=MESH,
        )

    def pair_copy(e, part, which):
        z = far(e)
        ref = xe_ref.at[z, halves(which), pl.ds(part * B, B)]
        return pltpu.make_async_remote_copy(
            src_ref=ref, dst_ref=ref, send_sem=pss.at[z, part], recv_sem=prs.at[z, part],
            device_id={"head": pair}, device_id_type=MESH,
        )

    def send_early(lo, hi):
        for j in range(lo, hi):
            if j % 2 == 1:
                x_copy(far(j // 2)).wait_recv()
            early_copy(j // 2, j % 2).start()

    def take_early(lo, hi):
        for j in range(lo, hi):
            early_copy(j // 2, j % 2).wait_recv()
            if paired:
                pair_copy(j // 2, j % 2, side).start()

    def have_early(lo, count):
        if paired:
            def one(e):
                for part in range(2):
                    pair_copy(lo + e, part, 1 - side).wait_recv()
            repeat(count, one)

    def partial(z, g):
        own = dot(xt_ref[share(z, dp), :], k_ref[:, columns(g)], 1, 0)
        return own + dot(xm_ref[z], gm_ref[:, columns(g)], 1, 0)

    def partial_extra(z, g):
        return partial(z, g) + dot(xe_ref[z], ge_ref[:, columns(g)], 1, 0)

    def term(z, g):
        down = (z < me).astype(jnp.int32)
        to = me + 1 - 2 * down
        slot = jnp.where((down == 1) & (to == z), n, z)
        return pltpu.make_async_remote_copy(
            src_ref=st_ref.at[z, g], dst_ref=st_ref.at[slot, g],
            send_sem=ss.at[z, g], recv_sem=rs.at[slot, g],
            device_id={"seq": to}, device_id_type=MESH,
        )

    def arrived(slot, g):
        pltpu.make_async_remote_copy(
            src_ref=st_ref.at[slot, g], dst_ref=st_ref.at[slot, g],
            send_sem=ss.at[0, g], recv_sem=rs.at[slot, g],
            device_id={"dp": mate}, device_id_type=MESH,
        ).wait_recv()

    def wait_x():
        @pl.when(inside)
        def _():
            lax.fori_loop(0, n, lambda z, c: (x_copy(z).wait_recv(), c)[1], 0)

        @pl.when(is_end)
        def _():
            x_copy(far(n - 1)).wait_recv()

    def take_factor(g):
        @pl.when(is_hub)
        def _():
            ends_copy(g).wait_recv()
            pass_copy(g).start()

    def send_share(e, g, before=None):
        z = far(e)
        pl.when(g == 0)(lambda: have_early(e, 1))
        if before is None:
            st_ref[z, g] = partial_extra(z, g).astype(BF16)
        else:
            near = dot(xe_ref[z, :, :B], ge_ref[:B, columns(g)], 1, 0)
            total = partial(z, g) + near
            before()
            total = total + dot(xe_ref[z, :, B:], ge_ref[B:, columns(g)], 1, 0)
            st_ref[z, g] = total.astype(BF16)
        term(z, g).start()

    def send_first(g):
        gk_copy(g).wait_recv()

        @pl.when(is_hub)
        def _():
            send_share(0, g, lambda: pass_copy(g).wait_recv())

    def send_rest(g):
        pl.when(is_hub)(lambda: repeat(late - 1, lambda e: send_share(e + 1, g)))

    def pass_on(z, g):
        total = partial(z, g)
        arrived(z, g)
        st_ref[z, g] = (total + st_ref[z, g].astype(F32)).astype(BF16)
        term(z, g).start()

    def send_on(g):
        pl.when(is_hub)(lambda: pass_on(ext, g))
        if n > 4:
            @pl.when(jnp.logical_not(is_hub | is_end))
            def _():
                def step(j, c):
                    z = (j // 2) * (1 - j % 2) + (n - 1 - j // 2) * (j % 2)
                    pl.when(z != me)(lambda: pass_on(z, g))
                    return c
                lax.fori_loop(0, n, step, 0)

    def guarded(cond, body):
        pl.when(cond)(body)

    pieces = 2 * late
    most = pieces * 3 // 4
    pl.when(upper & inside)(turn_inputs)
    greeted()
    for a in range(2, 4):
        load(a, 2).start()
    pl.when(upper & inside)(swap_inputs)

    @pl.when(me == n - 1)
    def _():
        if 2 * rows % LANES == 0:
            spans = 2 * rows // LANES

            def share_turn(e):
                z = far(e)
                lax.fori_loop(z * spans, (z + 1) * spans, turn, 0)
                x_copy(z).start()

            load_x.wait()
            share_turn(0)
            send_early(0, 1)
            lax.fori_loop(1, n, lambda e, c: (share_turn(e), c)[1], 0)
        else:
            turn_inputs()
            swap_inputs()
            send_early(0, 1)
        send_early(1, most)

    ahead = min(groups, 4)

    def prepare(g):
        update(g)
        guarded(g >= ahead, lambda: relay_forward(g - ahead))

        @pl.when(inside & jnp.logical_not(upper) & (g == min(ahead, groups - 1)))
        def _():
            turn_inputs()
            swap_inputs()

    each_group(prepare)
    make_mask()

    @pl.when(me == 0)
    def _():
        turn_inputs()
        swap_inputs()
        send_early(0, pieces)

    behind = jnp.where(me == 0, groups - 1, jnp.minimum((n - 2 - me) * 3 + 1, groups - 1))
    products = groups + 1

    def iteration(i, c):
        done = i - groups
        guarded(i < ahead, lambda: relay_forward(i + groups - ahead))
        guarded(i < groups, lambda: attention(i))

        for q in range(3):
            lo, hi = pieces * q // 4, pieces * (q + 1) // 4
            at = max(0, groups - 4 + 2 * q)
            guarded(is_hub & (i == at), lambda: take_early(lo, hi))
        guarded((me == n - 1) & (i == 1), lambda: send_early(most, pieces))
        guarded(is_end & (done == 5), lambda: send_early(pieces, pieces + 2))
        guarded((done >= 0) & (done < groups), lambda: grads(done))
        guarded(is_hub & (done == 1), lambda: take_early(pieces * 3 // 4, pieces))

        guarded(i == products, wait_x)

        ready = i - products
        guarded((ready >= 0) & (ready < groups), lambda: take_factor(ready))
        guarded((ready >= 0) & (ready < groups), lambda: send_first(ready))
        early = groups // 2
        guarded((ready >= 0) & (ready < early), lambda: send_rest(ready))
        guarded((ready > early) & (ready - 1 < groups), lambda: send_rest(ready - 1))
        guarded((ready >= 1) & (ready - 1 < groups), lambda: send_on(ready - 1))
        guarded(is_hub & (ready == 6), lambda: take_early(pieces, pieces + 2))
        guarded((i >= behind) & (i - behind < groups), lambda: relay_back(i - behind))
        return c

    lax.fori_loop(0, products + max(groups, 6) + 1, iteration, 0)

    def drain(g):
        @pl.when(me < n - 1)
        def _():
            forward(g).wait_send()

        @pl.when(me > 0)
        def _():
            backward(g).wait_send()

        gk_copy(g).wait_send()
        pl.when(is_end)(lambda: ends_copy(g).wait_send())
        pl.when(is_hub)(lambda: pass_copy(g).wait_send())

    each_group(drain)

    def sent_x(z, c):
        x_copy(z).wait_send()
        return c

    lax.fori_loop(0, n, sent_x, 0)

    def sent_early(e, c):
        for part in range(2):
            pl.when(is_end)(lambda: early_copy(e, part).wait_send())
            if paired:
                pl.when(is_hub)(lambda: pair_copy(e, part, side).wait_send())
        return c

    lax.fori_loop(0, n - 1, sent_early, 0)

    def settle(g):
        @pl.when(is_hub)
        def _():
            pl.when(g == 0)(lambda: have_early(late, 1))
            out_ref[:, columns(g)] = partial_extra(me, g)

        @pl.when(jnp.logical_not(is_hub))
        def _():
            out_ref[:, columns(g)] = partial(me, g)

        @pl.when(me > 1)
        def _():
            arrived(me, g)
            out_ref[:, columns(g)] += st_ref[me, g].astype(F32)

        @pl.when(me < n - 2)
        def _():
            arrived(n, g)
            out_ref[:, columns(g)] += st_ref[n, g].astype(F32)

        @pl.when(inside)
        def _():
            def step(z, c):
                pl.when(z != me)(lambda: term(z, g).wait_send())
                return c
            lax.fori_loop(0, n, step, 0)

    each_group(settle)


def layer(lengths, log_decay, x, q, k, v, g):
    heads, B = log_decay.shape
    D, F = x.shape[1], q.shape[1]
    n, group, groups, rows = sizes(heads, D)
    hbm = pl.BlockSpec(memory_space=pl.ANY)
    vmem = pl.BlockSpec(memory_space=pltpu.VMEM)
    state = (heads, LANES, LANES)
    wide = pltpu.VMEM((B, F), BF16)
    dma = pltpu.SemaphoreType.DMA
    return pl.pallas_call(
        functools.partial(layer_kernel, heads),
        out_shape=(wide, wide, pltpu.VMEM((rows, F), F32)),
        in_specs=[
            pl.BlockSpec(memory_space=pltpu.SMEM), pl.BlockSpec(memory_space=pltpu.VMEM)
        ] + [hbm] * 5,
        out_specs=(vmem, vmem, vmem),
        scratch_shapes=[pltpu.VMEM((B, F), BF16)] * 2
        + [
            pltpu.VMEM((B, D), BF16),
            pltpu.VMEM((D, B), BF16),
            pltpu.VMEM((n, rows, B), BF16),
            pltpu.VMEM((n, rows, 2 * B), BF16),
            pltpu.VMEM((B, F), BF16),
            pltpu.VMEM((2 * B, F), BF16),
            pltpu.VMEM((n + 1, groups, rows, group * LANES), BF16),
            pltpu.VMEM((heads, B), F32),
            pltpu.VMEM((heads, B, LANES), F32),
            pltpu.VMEM((B, B), F32),
            pltpu.VMEM((B, LANES), F32),
            pltpu.VMEM((B, LANES), F32),
            pltpu.VMEM(state, F32),
            pltpu.VMEM((heads, B, B), BF16),
            pltpu.VMEM((heads, B, LANES), BF16),
            pltpu.VMEM(state, F32),
        ]
        + [pltpu.VMEM(state, BF16)] * 4
        + [dma((groups,))] * 4
        + [
            dma((4, 2)), dma(()), dma((n,)), dma((n,)),
            dma((groups,)), dma((groups,)), dma((n, groups)), dma((n + 1, groups)),
        ]
        + [dma((n, 2))] * 4 + [dma((groups,))] * 4,
        compiler_params=pltpu.CompilerParams(
            collective_id=0, has_side_effects=True, vmem_limit_bytes=55 * 1024 * 1024
        ),
        name="layer",
    )(lengths, log_decay, x, q, k, v, g)


def deliver_kernel(*refs):
    count = (len(refs) - 1) // 2
    srcs, dsts, sem = refs[:count], refs[count:-1], refs[-1]
    moves = [pltpu.make_async_copy(srcs[a], dsts[a], sem.at[a]) for a in range(count)]
    for move in moves:
        move.start()
    for move in moves:
        move.wait()


def deliver(*arrays):
    hbm = pl.BlockSpec(memory_space=pl.ANY)
    vmem = pl.BlockSpec(memory_space=pltpu.VMEM)
    return pl.pallas_call(
        deliver_kernel,
        out_shape=tuple(jax.ShapeDtypeStruct(a.shape, a.dtype) for a in arrays),
        in_specs=[vmem] * len(arrays),
        out_specs=(hbm,) * len(arrays),
        scratch_shapes=[pltpu.SemaphoreType.DMA((len(arrays),))],
        compiler_params=pltpu.CompilerParams(vmem_limit_bytes=16 * 1024 * 1024),
        name="deliver",
    )(*arrays)


def body(inputs, queries, keys, values, log_decay, list_lengths, grad_out):
    gq, gv, gw = layer(
        list_lengths, log_decay[0], inputs[0], queries[0], keys[0], values[0], grad_out[0]
    )
    gq, gv, gw = deliver(gq, gv, gw)
    return gq[None], gv[None], gw


def solution(mesh):
    rows = ("groups", "dp")
    wide = P(rows, "seq", "head")
    return jax.shard_map(
        body,
        mesh=mesh,
        in_specs=(
            P(rows, "seq", None), wide, wide, wide, P(rows, "head", "seq"), P(rows, None), wide,
        ),
        out_specs=(wide, wide, P(("groups", "seq", "dp"), "head")),
        check_vma=False,
    )
```

```python
import functools
import math

import jax
import jax.numpy as jnp
from jax import lax
from jax.experimental import pallas as pl
from jax.experimental.pallas import tpu as pltpu
from jax.sharding import PartitionSpec as P

EPS = 1e-06
MESH = pl.DeviceIdType.MESH
LANES = 128
F32 = jnp.float32
BF16 = jnp.bfloat16


def dot(a, b, ca, cb):
    return lax.dot_general(a, b, (((ca,), (cb,)), ((), ())), preferred_element_type=F32)


def greet(pair):
    barrier = pltpu.get_barrier_semaphore()
    me = lax.axis_index("seq")
    n = lax.axis_size("seq")

    @pl.when(me > 0)
    def _():
        pl.semaphore_signal(barrier, inc=1, device_id={"seq": me - 1}, device_id_type=MESH)

    @pl.when(me < n - 1)
    def _():
        pl.semaphore_signal(barrier, inc=1, device_id={"seq": me + 1}, device_id_type=MESH)

    peers = (me > 0).astype(jnp.int32) + (me < n - 1).astype(jnp.int32) + 1
    mate = 1 - lax.axis_index("dp")
    pl.semaphore_signal(barrier, inc=1, device_id={"dp": mate}, device_id_type=MESH)
    if pair is not None:
        pl.semaphore_signal(barrier, inc=1, device_id={"head": pair}, device_id_type=MESH)
        peers = peers + 1
    return lambda: pl.semaphore_wait(barrier, peers)


def sizes(heads, D):
    group = math.gcd(heads, 2)
    n = lax.axis_size("seq")
    return n, group, heads // group, D // (2 * n)


def repeat(count, body):
    if count <= 3:
        for i in range(count):
            body(i)
        return

    def step(i, c):
        body(i)
        return c

    lax.fori_loop(0, count, step, 0)


def layer_kernel(
    heads, ll_ref, ld_ref, x_hbm, q_hbm, k_hbm, v_hbm, g_hbm, q_ref, g_ref, out_ref,
    k_ref, v_ref, x_ref, xt_ref, xm_ref, xe_ref, gm_ref, ge_ref, st_ref,
    cum_ref, colb_ref, mask_ref, min_ref, mout_ref, upd_ref, sc_ref, ga_ref,
    bs_ref, fsend, frecv, bsend, brecv, fss, frs, bss, brs,
    load_sem, x_sem, xss, xrs, gss, grs, ss, rs, ess, ers, pss, prs, hss, hrs, mss, mrs,
):
    me = lax.axis_index("seq")
    dp = lax.axis_index("dp")
    hx = lax.axis_index("head")
    B, D = x_ref.shape
    n, group, groups, rows = sizes(heads, D)
    first = me * B
    mate = 1 - dp
    width = group * LANES
    paired = lax.axis_size("head") % 2 == 0
    half = rows // 2 if paired else rows
    side = hx % 2 if paired else 0
    pair = hx + 1 - 2 * side if paired else None
    late = n - 2

    is_end = (me == 0) | (me == n - 1)
    is_hub = (me == 1) | (me == n - 2)
    inside = jnp.logical_not(is_end)
    low = me <= 1
    hub = jnp.where(low, 1, n - 2)
    ext = jnp.where(low, 0, n - 1)

    def far(e):
        return jnp.where(low, n - 1 - e, e)

    def columns(g):
        return pl.ds(pl.multiple_of(g * width, LANES), width)

    def load(a, part):
        src = (k_hbm, v_hbm, q_hbm, g_hbm)[a]
        dst = (k_ref, v_ref, q_ref, g_ref)[a]
        cols = (slice(0, width), slice(width, heads * LANES), slice(0, heads * LANES))[part]
        return pltpu.make_async_copy(src.at[:, cols], dst.at[:, cols], load_sem.at[a, min(part, 1)])

    def each_group(body, start=0):
        def step(g, c):
            body(g)
            return c
        lax.fori_loop(start, groups, step, 0)

    greeted = greet(pair)

    load_x = pltpu.make_async_copy(x_hbm, x_ref, x_sem)
    upper = 2 * me >= n
    pl.when(upper)(load_x.start)
    for a in range(2):
        load(a, 0).start()
    pl.when(jnp.logical_not(upper))(load_x.start)
    for a in range(2):
        load(a, 1).start()

    lengths = [ll_ref[0, i] for i in range(ll_ref.shape[1])]
    starts = [jnp.int32(0)]
    for length in lengths[:-1]:
        starts.append(starts[-1] + length)

    def seg_of(pos):
        total = (starts[0] <= pos).astype(jnp.int32)
        for s in starts[1:]:
            total = total + (s <= pos).astype(jnp.int32)
        return total

    before = seg_of(first - 1)
    end = seg_of(first + B - 1)
    seg_col = seg_of(first + lax.broadcasted_iota(jnp.int32, (B, LANES), 0))
    min_ref[...] = jnp.where(seg_col == before, 1.0, 0.0).astype(F32)
    mout_ref[...] = jnp.where(seg_col == end, 1.0, 0.0).astype(F32)
    open_all = jnp.where(jnp.full((1, LANES), end) == before, 1.0, 0.0).astype(F32)
    above = lax.broadcasted_iota(jnp.int32, (LANES, LANES), 0)
    below = lax.broadcasted_iota(jnp.int32, (LANES, LANES), 1)
    tri = jnp.where(above <= below, 1.0, 0.0).astype(F32)
    carry = jnp.zeros((heads, 1), F32)
    for c in range(B // LANES):
        span = slice(c * LANES, (c + 1) * LANES)
        run = carry + lax.dot_general(
            ld_ref[:, span], tri, (((1,), (0,)), ((), ())),
            preferred_element_type=F32, precision=lax.Precision.HIGHEST,
        )
        cum_ref[:, span] = run
        carry = run[:, LANES - 1 :]

    def make_mask():
        t_pos = lax.broadcasted_iota(jnp.int32, (B, B), 0)
        u_pos = lax.broadcasted_iota(jnp.int32, (B, B), 1)
        wide = jnp.concatenate([seg_col] * (B // LANES), axis=1)
        row = seg_of(first + lax.broadcasted_iota(jnp.int32, (1, B), 1))
        same = (t_pos >= u_pos) & (wide == row)
        mask_ref[...] = jnp.where(same, 0.0, -1e30).astype(F32)

    def lanes(h):
        return pl.ds(pl.multiple_of(h * LANES, LANES), LANES)

    def weight_of(h):
        cb = colb_ref[h]
        return jnp.exp(cb[B - 1 : B, :] - cb) * mout_ref[...]

    def gamma_of(h):
        return jnp.exp(colb_ref[h]) * min_ref[...]

    def passing_of(h):
        return jnp.exp(colb_ref[h, B - 1 : B, :]) * open_all

    def decay_of(h, ts, cols):
        cb = colb_ref[h, ts, :]
        wide = jnp.concatenate([cb] * (cols // LANES), axis=1)
        row = cum_ref[pl.ds(h, 1), :cols]
        return jnp.exp((wide - row) + mask_ref[ts, :cols])

    def each_head(g, body):
        for i in range(group):
            body(g * group + i, i)

    def hop(src, dst, ss, rs, g, to):
        span = pl.ds(g * group, group)
        return pltpu.make_async_remote_copy(
            src_ref=src.at[span], dst_ref=dst.at[span], send_sem=ss.at[g], recv_sem=rs.at[g],
            device_id={"seq": to}, device_id_type=MESH,
        )

    def forward(g):
        return hop(fsend, frecv, fss, frs, g, me + 1)

    def backward(g):
        return hop(bsend, brecv, bss, brs, g, me - 1)

    def update_work(g):
        for part in range(2):
            @pl.when(g == part)
            def _():
                load(0, part).wait()
                load(1, part).wait()

        def column(h, i):
            colb_ref[h] = jnp.transpose(jnp.broadcast_to(cum_ref[pl.ds(h, 1), :], (LANES, B)))

        def one(h, i):
            column(h, i)
            wk = (k_ref[:, lanes(h)].astype(F32) * weight_of(h)).astype(BF16)
            upd_ref[h] = dot(wk, v_ref[:, lanes(h)], 0, 0)

        pl.when(me == n - 1)(lambda: each_head(g, column))
        pl.when(me < n - 1)(lambda: each_head(g, one))

    def update_send(g):
        @pl.when(me == 0)
        def _():
            def ready(h, i):
                fsend[h] = upd_ref[h].astype(BF16)
                frecv[h] = jnp.zeros((LANES, LANES), BF16)
            each_head(g, ready)
            forward(g).start()

        @pl.when(me == n - 1)
        def _():
            def ready(h, i):
                brecv[h] = jnp.zeros((LANES, LANES), BF16)
            each_head(g, ready)

    def relay_forward(g):
        @pl.when(inside)
        def _():
            forward(g).wait_recv()

            def send(h, i):
                fsend[h] = (passing_of(h) * frecv[h].astype(F32) + upd_ref[h]).astype(BF16)
            each_head(g, send)
            forward(g).start()

    def attention(g):
        @pl.when(g == 0)
        def _():
            load(2, 2).wait()
            load(3, 2).wait()

        @pl.when(me == n - 1)
        def _():
            forward(g).wait_recv()

        def one(h, i):
            q = q_ref[:, lanes(h)]
            s = dot(q, k_ref[:, lanes(h)], 1, 1)
            s_bf = (s * decay_of(h, slice(0, B), B)).astype(BF16)
            sc_ref[h] = s_bf
            gamma = gamma_of(h)
            att = gamma * dot(q, frecv[h], 1, 0) + dot(s_bf, v_ref[:, lanes(h)], 1, 0)
            inv = lax.rsqrt(jnp.mean(att * att, axis=-1, keepdims=True) + EPS)
            normed = att * inv
            wide = g_ref[:, lanes(h)].astype(F32)
            ga = (inv * (wide - normed * jnp.mean(wide * normed, axis=-1, keepdims=True))).astype(BF16)
            ga_ref[h] = ga
            gated = (q.astype(F32) * gamma).astype(BF16)
            bs_ref[h] = dot(gated, ga, 0, 0)

        each_head(g, one)

        @pl.when(me == n - 1)
        def _():
            def ready(h, i):
                bsend[h] = bs_ref[h].astype(BF16)
            each_head(g, ready)
            backward(g).start()

    def relay_back(g):
        @pl.when(me < n - 1)
        def _():
            backward(g).wait_recv()

        @pl.when(inside)
        def _():
            def send(h, i):
                bsend[h] = (passing_of(h) * brecv[h].astype(F32) + bs_ref[h]).astype(BF16)
            each_head(g, send)
            backward(g).start()

    tile = math.gcd(B, 256)
    tiles = B // tile

    def grads(g):
        def one(h, i):
            gamma = gamma_of(h)
            w = weight_of(h)
            later = brecv[h]
            kis, vis = [None] * tiles, [None] * tiles
            for b in range(tiles):
                ts, cols = slice(b * tile, (b + 1) * tile), (b + 1) * tile
                ga = ga_ref[h, ts, :]
                q = q_ref[ts, lanes(h)]
                gs = (dot(ga, v_ref[:cols, lanes(h)], 1, 1) * decay_of(h, ts, cols)).astype(BF16)
                gq = gamma[ts] * dot(ga, frecv[h], 1, 1) + dot(gs, k_ref[:cols, lanes(h)], 1, 0)
                ki = dot(gs, q, 0, 0)
                vi = dot(sc_ref[h, ts, :cols], ga, 0, 0)
                q_ref[ts, lanes(h)] = gq.astype(BF16)
                for j in range(b + 1):
                    js = slice(j * tile, (j + 1) * tile)
                    kis[j] = ki[js] if kis[j] is None else kis[j] + ki[js]
                    vis[j] = vi[js] if vis[j] is None else vis[j] + vi[js]
            for j in range(tiles):
                js = slice(j * tile, (j + 1) * tile)
                k = k_ref[js, lanes(h)]
                gk = kis[j] + w[js] * dot(v_ref[js, lanes(h)], later, 1, 1)
                gv = vis[j] + w[js] * dot(k, later, 1, 0)
                k_ref[js, lanes(h)] = gk.astype(BF16)
                g_ref[js, lanes(h)] = gv.astype(BF16)

        each_head(g, one)
        pl.when(is_end)(lambda: ends_copy(g).start())
        gk_copy(g).start()

    def gk_copy(g):
        return pltpu.make_async_remote_copy(
            src_ref=k_ref.at[:, columns(g)], dst_ref=gm_ref.at[:, columns(g)],
            send_sem=gss.at[g], recv_sem=grs.at[g],
            device_id={"dp": mate}, device_id_type=MESH,
        )

    def ends_copy(g):
        return pltpu.make_async_remote_copy(
            src_ref=k_ref.at[:, columns(g)], dst_ref=ge_ref.at[pl.ds(0, B), columns(g)],
            send_sem=hss.at[g], recv_sem=hrs.at[g],
            device_id={"seq": hub}, device_id_type=MESH,
        )

    def pass_copy(g):
        return pltpu.make_async_remote_copy(
            src_ref=ge_ref.at[pl.ds(0, B), columns(g)], dst_ref=ge_ref.at[pl.ds(B, B), columns(g)],
            send_sem=mss.at[g], recv_sem=mrs.at[g],
            device_id={"dp": mate}, device_id_type=MESH,
        )

    def share(z, owner):
        return pl.ds(pl.multiple_of((z * 2 + owner) * rows, math.gcd(rows, LANES)), rows)

    def halves(which, base=0):
        return pl.ds(pl.multiple_of(base + which * half, math.gcd(half, LANES)), half)

    def x_copy(z):
        return pltpu.make_async_remote_copy(
            src_ref=xt_ref.at[share(z, mate)], dst_ref=xm_ref.at[z],
            send_sem=xss.at[z], recv_sem=xrs.at[z],
            device_id={"dp": mate}, device_id_type=MESH,
        )

    def turn(i, c):
        span = pl.ds(pl.multiple_of(i * LANES, LANES), LANES)
        xt_ref[span, :] = jnp.transpose(x_ref[:, span])
        return c

    def turn_inputs():
        load_x.wait()
        lax.fori_loop(0, D // LANES, turn, 0)

    def swap_inputs():
        lax.fori_loop(0, n, lambda e, c: (x_copy(far(e)).start(), c)[1], 0)

    def early_copy(e, part):
        z = far(e)
        src = (
            xt_ref.at[halves(side, (z * 2 + dp) * rows)] if part == 0 else xm_ref.at[z, halves(side)]
        )
        return pltpu.make_async_remote_copy(
            src_ref=src, dst_ref=xe_ref.at[z, halves(side), pl.ds(part * B, B)],
            send_sem=ess.at[z, part], recv_sem=ers.at[z, part],
            device_id={"seq": hub}, device_id_type=MESH,
        )

    def pair_copy(e, part, which):
        z = far(e)
        ref = xe_ref.at[z, halves(which), pl.ds(part * B, B)]
        return pltpu.make_async_remote_copy(
            src_ref=ref, dst_ref=ref, send_sem=pss.at[z, part], recv_sem=prs.at[z, part],
            device_id={"head": pair}, device_id_type=MESH,
        )

    def send_early(lo, hi):
        for j in range(lo, hi):
            if j % 2 == 1:
                x_copy(far(j // 2)).wait_recv()
            early_copy(j // 2, j % 2).start()

    def take_early(lo, hi):
        for j in range(lo, hi):
            early_copy(j // 2, j % 2).wait_recv()
            if paired:
                pair_copy(j // 2, j % 2, side).start()

    def have_early(lo, count):
        if paired:
            def one(e):
                for part in range(2):
                    pair_copy(lo + e, part, 1 - side).wait_recv()
            repeat(count, one)

    def partial(z, g):
        own = dot(xt_ref[share(z, dp), :], k_ref[:, columns(g)], 1, 0)
        return own + dot(xm_ref[z], gm_ref[:, columns(g)], 1, 0)

    def partial_extra(z, g):
        return partial(z, g) + dot(xe_ref[z], ge_ref[:, columns(g)], 1, 0)

    def term(z, g):
        down = (z < me).astype(jnp.int32)
        to = me + 1 - 2 * down
        slot = jnp.where((down == 1) & (to == z), n, z)
        return pltpu.make_async_remote_copy(
            src_ref=st_ref.at[z, g], dst_ref=st_ref.at[slot, g],
            send_sem=ss.at[z, g], recv_sem=rs.at[slot, g],
            device_id={"seq": to}, device_id_type=MESH,
        )

    def arrived(slot, g):
        pltpu.make_async_remote_copy(
            src_ref=st_ref.at[slot, g], dst_ref=st_ref.at[slot, g],
            send_sem=ss.at[0, g], recv_sem=rs.at[slot, g],
            device_id={"dp": mate}, device_id_type=MESH,
        ).wait_recv()

    def wait_x():
        @pl.when(inside)
        def _():
            lax.fori_loop(0, n, lambda z, c: (x_copy(z).wait_recv(), c)[1], 0)

        @pl.when(is_end)
        def _():
            x_copy(far(n - 1)).wait_recv()

    def take_factor(g):
        @pl.when(is_hub)
        def _():
            ends_copy(g).wait_recv()
            pass_copy(g).start()

    def send_share(e, g):
        z = far(e)
        pl.when(g == 0)(lambda: have_early(e, 1))
        st_ref[z, g] = partial_extra(z, g).astype(BF16)
        term(z, g).start()

    def send_first(g):
        gk_copy(g).wait_recv()

        @pl.when(is_hub)
        def _():
            pass_copy(g).wait_recv()
            send_share(0, g)

    def send_rest(g):
        pl.when(is_hub)(lambda: repeat(late - 1, lambda e: send_share(e + 1, g)))

    def pass_on(z, g):
        total = partial(z, g)
        arrived(z, g)
        st_ref[z, g] = (total + st_ref[z, g].astype(F32)).astype(BF16)
        term(z, g).start()

    def send_on(g):
        pl.when(is_hub)(lambda: pass_on(ext, g))
        if n > 4:
            @pl.when(jnp.logical_not(is_hub | is_end))
            def _():
                def step(j, c):
                    z = (j // 2) * (1 - j % 2) + (n - 1 - j // 2) * (j % 2)
                    pl.when(z != me)(lambda: pass_on(z, g))
                    return c
                lax.fori_loop(0, n, step, 0)

    def guarded(cond, body):
        pl.when(cond)(body)

    pieces = 2 * late
    most = pieces * 3 // 4
    even = 2 * rows % LANES == 0
    spans = 2 * rows // LANES

    def share_turn(e):
        z = far(e)
        lax.fori_loop(z * spans, (z + 1) * spans, turn, 0)

    @pl.when(me == n - 1)
    def _():
        if even:
            load_x.wait()
            share_turn(0)
        else:
            turn_inputs()

    pl.when(upper & inside)(turn_inputs)
    update_work(jnp.int32(0))
    greeted()

    @pl.when(me == n - 1)
    def _():
        x_copy(far(0)).start()
        send_early(0, 1)

        def step(e, c):
            if even:
                share_turn(e)
            x_copy(far(e)).start()
            return c

        lax.fori_loop(1, n, step, 0)
        send_early(1, most)

    for a in range(2, 4):
        load(a, 2).start()
    pl.when(upper & inside)(swap_inputs)

    ahead = min(groups, 4)

    def prepare(g):
        pl.when(g > 0)(lambda: update_work(g))
        update_send(g)
        guarded(g >= ahead, lambda: relay_forward(g - ahead))

        @pl.when(inside & jnp.logical_not(upper) & (g == min(ahead, groups - 1)))
        def _():
            turn_inputs()
            swap_inputs()

    each_group(prepare)
    make_mask()

    @pl.when(me == 0)
    def _():
        turn_inputs()
        swap_inputs()
        send_early(0, pieces)

    behind = jnp.where(me == 0, groups - 1, jnp.minimum((n - 2 - me) * 3 + 1, groups - 1))
    products = groups + 1

    def iteration(i, c):
        done = i - groups
        guarded(i < ahead, lambda: relay_forward(i + groups - ahead))
        guarded(i < groups, lambda: attention(i))

        for q in range(3):
            lo, hi = pieces * q // 4, pieces * (q + 1) // 4
            at = max(0, groups - 4 + 2 * q)
            guarded(is_hub & (i == at), lambda: take_early(lo, hi))
        guarded((me == n - 1) & (i == 1), lambda: send_early(most, pieces))
        guarded(is_end & (done == 5), lambda: send_early(pieces, pieces + 2))
        guarded((done >= 0) & (done < groups), lambda: grads(done))
        guarded(is_hub & (done == 1), lambda: take_early(pieces * 3 // 4, pieces))

        guarded(i == products, wait_x)

        ready = i - products
        guarded((ready >= 1) & (ready <= groups // 2), lambda: send_rest(ready - 1))
        guarded((ready >= 0) & (ready < groups), lambda: take_factor(ready))
        guarded((ready >= 0) & (ready < groups), lambda: send_first(ready))
        guarded((ready > groups // 2) & (ready - 1 < groups), lambda: send_rest(ready - 1))
        guarded((ready >= 1) & (ready - 1 < groups), lambda: send_on(ready - 1))
        guarded(is_hub & (ready == 6), lambda: take_early(pieces, pieces + 2))
        guarded((i >= behind) & (i - behind < groups), lambda: relay_back(i - behind))
        return c

    lax.fori_loop(0, products + max(groups, 6) + 1, iteration, 0)

    def drain(g):
        @pl.when(me < n - 1)
        def _():
            forward(g).wait_send()

        @pl.when(me > 0)
        def _():
            backward(g).wait_send()

        gk_copy(g).wait_send()
        pl.when(is_end)(lambda: ends_copy(g).wait_send())
        pl.when(is_hub)(lambda: pass_copy(g).wait_send())

    each_group(drain)

    def sent_x(z, c):
        x_copy(z).wait_send()
        return c

    lax.fori_loop(0, n, sent_x, 0)

    def sent_early(e, c):
        for part in range(2):
            pl.when(is_end)(lambda: early_copy(e, part).wait_send())
            if paired:
                pl.when(is_hub)(lambda: pair_copy(e, part, side).wait_send())
        return c

    lax.fori_loop(0, n - 1, sent_early, 0)

    def settle(g):
        @pl.when(is_hub)
        def _():
            pl.when(g == 0)(lambda: have_early(late, 1))
            out_ref[:, columns(g)] = partial_extra(me, g)

        @pl.when(jnp.logical_not(is_hub))
        def _():
            out_ref[:, columns(g)] = partial(me, g)

        @pl.when(me > 1)
        def _():
            arrived(me, g)
            out_ref[:, columns(g)] += st_ref[me, g].astype(F32)

        @pl.when(me < n - 2)
        def _():
            arrived(n, g)
            out_ref[:, columns(g)] += st_ref[n, g].astype(F32)

        @pl.when(inside)
        def _():
            def step(z, c):
                pl.when(z != me)(lambda: term(z, g).wait_send())
                return c
            lax.fori_loop(0, n, step, 0)

    each_group(settle)


def layer(lengths, log_decay, x, q, k, v, g):
    heads, B = log_decay.shape
    D, F = x.shape[1], q.shape[1]
    n, group, groups, rows = sizes(heads, D)
    hbm = pl.BlockSpec(memory_space=pl.ANY)
    vmem = pl.BlockSpec(memory_space=pltpu.VMEM)
    state = (heads, LANES, LANES)
    wide = pltpu.VMEM((B, F), BF16)
    dma = pltpu.SemaphoreType.DMA
    return pl.pallas_call(
        functools.partial(layer_kernel, heads),
        out_shape=(wide, wide, pltpu.VMEM((rows, F), F32)),
        in_specs=[
            pl.BlockSpec(memory_space=pltpu.SMEM), pl.BlockSpec(memory_space=pltpu.VMEM)
        ] + [hbm] * 5,
        out_specs=(vmem, vmem, vmem),
        scratch_shapes=[pltpu.VMEM((B, F), BF16)] * 2
        + [
            pltpu.VMEM((B, D), BF16),
            pltpu.VMEM((D, B), BF16),
            pltpu.VMEM((n, rows, B), BF16),
            pltpu.VMEM((n, rows, 2 * B), BF16),
            pltpu.VMEM((B, F), BF16),
            pltpu.VMEM((2 * B, F), BF16),
            pltpu.VMEM((n + 1, groups, rows, group * LANES), BF16),
            pltpu.VMEM((heads, B), F32),
            pltpu.VMEM((heads, B, LANES), F32),
            pltpu.VMEM((B, B), F32),
            pltpu.VMEM((B, LANES), F32),
            pltpu.VMEM((B, LANES), F32),
            pltpu.VMEM(state, F32),
            pltpu.VMEM((heads, B, B), BF16),
            pltpu.VMEM((heads, B, LANES), BF16),
            pltpu.VMEM(state, F32),
        ]
        + [pltpu.VMEM(state, BF16)] * 4
        + [dma((groups,))] * 4
        + [
            dma((4, 2)), dma(()), dma((n,)), dma((n,)),
            dma((groups,)), dma((groups,)), dma((n, groups)), dma((n + 1, groups)),
        ]
        + [dma((n, 2))] * 4 + [dma((groups,))] * 4,
        compiler_params=pltpu.CompilerParams(
            collective_id=0, has_side_effects=True, vmem_limit_bytes=55 * 1024 * 1024
        ),
        name="layer",
    )(lengths, log_decay, x, q, k, v, g)


def deliver_kernel(*refs):
    count = (len(refs) - 1) // 2
    srcs, dsts, sem = refs[:count], refs[count:-1], refs[-1]
    moves = [pltpu.make_async_copy(srcs[a], dsts[a], sem.at[a]) for a in range(count)]
    for move in moves:
        move.start()
    for move in moves:
        move.wait()


def deliver(*arrays):
    hbm = pl.BlockSpec(memory_space=pl.ANY)
    vmem = pl.BlockSpec(memory_space=pltpu.VMEM)
    return pl.pallas_call(
        deliver_kernel,
        out_shape=tuple(jax.ShapeDtypeStruct(a.shape, a.dtype) for a in arrays),
        in_specs=[vmem] * len(arrays),
        out_specs=(hbm,) * len(arrays),
        scratch_shapes=[pltpu.SemaphoreType.DMA((len(arrays),))],
        compiler_params=pltpu.CompilerParams(vmem_limit_bytes=16 * 1024 * 1024),
        name="deliver",
    )(*arrays)


def body(inputs, queries, keys, values, log_decay, list_lengths, grad_out):
    gq, gv, gw = layer(
        list_lengths, log_decay[0], inputs[0], queries[0], keys[0], values[0], grad_out[0]
    )
    gq, gv, gw = deliver(gq, gv, gw)
    return gq[None], gv[None], gw


def solution(mesh):
    rows = ("groups", "dp")
    wide = P(rows, "seq", "head")
    return jax.shard_map(
        body,
        mesh=mesh,
        in_specs=(
            P(rows, "seq", None), wide, wide, wide, P(rows, "head", "seq"), P(rows, None), wide,
        ),
        out_specs=(wide, wide, P(("groups", "seq", "dp"), "head")),
        check_vma=False,
    )
```

```python
import functools
import math

import jax
import jax.numpy as jnp
from jax import lax
from jax.experimental import pallas as pl
from jax.experimental.pallas import tpu as pltpu
from jax.sharding import PartitionSpec as P

EPS = 1e-06
MESH = pl.DeviceIdType.MESH
LANES = 128
F32 = jnp.float32
BF16 = jnp.bfloat16


def dot(a, b, ca, cb):
    return lax.dot_general(a, b, (((ca,), (cb,)), ((), ())), preferred_element_type=F32)


def greet(pair):
    barrier = pltpu.get_barrier_semaphore()
    me = lax.axis_index("seq")
    n = lax.axis_size("seq")

    @pl.when(me > 0)
    def _():
        pl.semaphore_signal(barrier, inc=1, device_id={"seq": me - 1}, device_id_type=MESH)

    @pl.when(me < n - 1)
    def _():
        pl.semaphore_signal(barrier, inc=1, device_id={"seq": me + 1}, device_id_type=MESH)

    peers = (me > 0).astype(jnp.int32) + (me < n - 1).astype(jnp.int32) + 1
    mate = 1 - lax.axis_index("dp")
    pl.semaphore_signal(barrier, inc=1, device_id={"dp": mate}, device_id_type=MESH)
    if pair is not None:
        pl.semaphore_signal(barrier, inc=1, device_id={"head": pair}, device_id_type=MESH)
        peers = peers + 1
    return lambda: pl.semaphore_wait(barrier, peers)


def sizes(heads, D):
    group = math.gcd(heads, 2)
    n = lax.axis_size("seq")
    return n, group, heads // group, D // (2 * n)


def repeat(count, body):
    if count <= 3:
        for i in range(count):
            body(i)
        return

    def step(i, c):
        body(i)
        return c

    lax.fori_loop(0, count, step, 0)


def layer_kernel(
    heads, ll_ref, ld_ref, x_hbm, q_hbm, k_hbm, v_hbm, g_hbm, q_ref, g_ref, out_ref,
    k_ref, v_ref, x_ref, xt_ref, xm_ref, xe_ref, gm_ref, ge_ref, st_ref,
    cum_ref, colb_ref, mask_ref, min_ref, mout_ref, upd_ref, sc_ref, ga_ref,
    bs_ref, fsend, frecv, bsend, brecv, fss, frs, bss, brs,
    load_sem, x_sem, xss, xrs, gss, grs, ss, rs, ess, ers, pss, prs, hss, hrs, mss, mrs,
):
    me = lax.axis_index("seq")
    dp = lax.axis_index("dp")
    hx = lax.axis_index("head")
    B, D = x_ref.shape
    n, group, groups, rows = sizes(heads, D)
    first = me * B
    mate = 1 - dp
    width = group * LANES
    paired = lax.axis_size("head") % 2 == 0
    half = rows // 2 if paired else rows
    side = hx % 2 if paired else 0
    pair = hx + 1 - 2 * side if paired else None
    late = n - 2

    is_end = (me == 0) | (me == n - 1)
    is_hub = (me == 1) | (me == n - 2)
    inside = jnp.logical_not(is_end)
    low = me <= 1
    hub = jnp.where(low, 1, n - 2)
    ext = jnp.where(low, 0, n - 1)

    def far(e):
        return jnp.where(low, n - 1 - e, e)

    def columns(g):
        return pl.ds(pl.multiple_of(g * width, LANES), width)

    def load(a, part):
        src = (k_hbm, v_hbm, q_hbm, g_hbm)[a]
        dst = (k_ref, v_ref, q_ref, g_ref)[a]
        cols = (slice(0, width), slice(width, heads * LANES), slice(0, heads * LANES))[part]
        return pltpu.make_async_copy(src.at[:, cols], dst.at[:, cols], load_sem.at[a, min(part, 1)])

    def each_group(body, start=0):
        def step(g, c):
            body(g)
            return c
        lax.fori_loop(start, groups, step, 0)

    greeted = greet(pair)

    load_x = pltpu.make_async_copy(x_hbm, x_ref, x_sem)
    upper = 2 * me >= n
    pl.when(upper)(load_x.start)
    for a in range(2):
        load(a, 0).start()
    pl.when(jnp.logical_not(upper))(load_x.start)
    for a in range(2):
        load(a, 1).start()

    lengths = [ll_ref[0, i] for i in range(ll_ref.shape[1])]
    starts = [jnp.int32(0)]
    for length in lengths[:-1]:
        starts.append(starts[-1] + length)

    def seg_of(pos):
        total = (starts[0] <= pos).astype(jnp.int32)
        for s in starts[1:]:
            total = total + (s <= pos).astype(jnp.int32)
        return total

    before = seg_of(first - 1)
    end = seg_of(first + B - 1)
    seg_col = seg_of(first + lax.broadcasted_iota(jnp.int32, (B, LANES), 0))
    min_ref[...] = jnp.where(seg_col == before, 1.0, 0.0).astype(F32)
    mout_ref[...] = jnp.where(seg_col == end, 1.0, 0.0).astype(F32)
    open_all = jnp.where(jnp.full((1, LANES), end) == before, 1.0, 0.0).astype(F32)
    above = lax.broadcasted_iota(jnp.int32, (LANES, LANES), 0)
    below = lax.broadcasted_iota(jnp.int32, (LANES, LANES), 1)
    tri = jnp.where(above <= below, 1.0, 0.0).astype(F32)
    carry = jnp.zeros((heads, 1), F32)
    for c in range(B // LANES):
        span = slice(c * LANES, (c + 1) * LANES)
        run = carry + lax.dot_general(
            ld_ref[:, span], tri, (((1,), (0,)), ((), ())),
            preferred_element_type=F32, precision=lax.Precision.HIGHEST,
        )
        cum_ref[:, span] = run
        carry = run[:, LANES - 1 :]

    def make_mask():
        t_pos = lax.broadcasted_iota(jnp.int32, (B, B), 0)
        u_pos = lax.broadcasted_iota(jnp.int32, (B, B), 1)
        wide = jnp.concatenate([seg_col] * (B // LANES), axis=1)
        row = seg_of(first + lax.broadcasted_iota(jnp.int32, (1, B), 1))
        same = (t_pos >= u_pos) & (wide == row)
        mask_ref[...] = jnp.where(same, 0.0, -1e30).astype(F32)

    def lanes(h):
        return pl.ds(pl.multiple_of(h * LANES, LANES), LANES)

    def weight_of(h):
        cb = colb_ref[h]
        return jnp.exp(cb[B - 1 : B, :] - cb) * mout_ref[...]

    def gamma_of(h):
        return jnp.exp(colb_ref[h]) * min_ref[...]

    def passing_of(h):
        return jnp.exp(colb_ref[h, B - 1 : B, :]) * open_all

    def decay_of(h, ts, cols):
        cb = colb_ref[h, ts, :]
        wide = jnp.concatenate([cb] * (cols // LANES), axis=1)
        row = cum_ref[pl.ds(h, 1), :cols]
        return jnp.exp((wide - row) + mask_ref[ts, :cols])

    def each_head(g, body):
        for i in range(group):
            body(g * group + i, i)

    def hop(src, dst, ss, rs, g, to):
        span = pl.ds(g * group, group)
        return pltpu.make_async_remote_copy(
            src_ref=src.at[span], dst_ref=dst.at[span], send_sem=ss.at[g], recv_sem=rs.at[g],
            device_id={"seq": to}, device_id_type=MESH,
        )

    def forward(g):
        return hop(fsend, frecv, fss, frs, g, me + 1)

    def backward(g):
        return hop(bsend, brecv, bss, brs, g, me - 1)

    def update(g):
        for part in range(2):
            @pl.when(g == part)
            def _():
                load(0, part).wait()
                load(1, part).wait()

        def column(h, i):
            colb_ref[h] = jnp.transpose(jnp.broadcast_to(cum_ref[pl.ds(h, 1), :], (LANES, B)))

        def one(h, i):
            column(h, i)
            wk = (k_ref[:, lanes(h)].astype(F32) * weight_of(h)).astype(BF16)
            upd_ref[h] = dot(wk, v_ref[:, lanes(h)], 0, 0)

        pl.when(me == n - 1)(lambda: each_head(g, column))
        pl.when(me < n - 1)(lambda: each_head(g, one))

        @pl.when(me == 0)
        def _():
            def ready(h, i):
                fsend[h] = upd_ref[h].astype(BF16)
                frecv[h] = jnp.zeros((LANES, LANES), BF16)
            each_head(g, ready)
            forward(g).start()

        @pl.when(me == n - 1)
        def _():
            def ready(h, i):
                brecv[h] = jnp.zeros((LANES, LANES), BF16)
            each_head(g, ready)

    def relay_forward(g):
        @pl.when(inside)
        def _():
            forward(g).wait_recv()

            def send(h, i):
                fsend[h] = (passing_of(h) * frecv[h].astype(F32) + upd_ref[h]).astype(BF16)
            each_head(g, send)
            forward(g).start()

    def attention(g):
        @pl.when(g == 0)
        def _():
            load(2, 2).wait()
            load(3, 2).wait()

        @pl.when(me == n - 1)
        def _():
            forward(g).wait_recv()

        def one(h, i):
            q = q_ref[:, lanes(h)]
            s = dot(q, k_ref[:, lanes(h)], 1, 1)
            s_bf = (s * decay_of(h, slice(0, B), B)).astype(BF16)
            sc_ref[h] = s_bf
            gamma = gamma_of(h)
            att = gamma * dot(q, frecv[h], 1, 0) + dot(s_bf, v_ref[:, lanes(h)], 1, 0)
            inv = lax.rsqrt(jnp.mean(att * att, axis=-1, keepdims=True) + EPS)
            normed = att * inv
            wide = g_ref[:, lanes(h)].astype(F32)
            ga = (inv * (wide - normed * jnp.mean(wide * normed, axis=-1, keepdims=True))).astype(BF16)
            ga_ref[h] = ga
            gated = (q.astype(F32) * gamma).astype(BF16)
            bs_ref[h] = dot(gated, ga, 0, 0)

        each_head(g, one)

        @pl.when(me == n - 1)
        def _():
            def ready(h, i):
                bsend[h] = bs_ref[h].astype(BF16)
            each_head(g, ready)
            backward(g).start()

    def relay_back(g):
        @pl.when(me < n - 1)
        def _():
            backward(g).wait_recv()

        @pl.when(inside)
        def _():
            def send(h, i):
                bsend[h] = (passing_of(h) * brecv[h].astype(F32) + bs_ref[h]).astype(BF16)
            each_head(g, send)
            backward(g).start()

    tile = math.gcd(B, 256)
    tiles = B // tile

    def grads(g):
        def one(h, i):
            gamma = gamma_of(h)
            w = weight_of(h)
            later = brecv[h]
            kis, vis = [None] * tiles, [None] * tiles
            for b in range(tiles):
                ts, cols = slice(b * tile, (b + 1) * tile), (b + 1) * tile
                ga = ga_ref[h, ts, :]
                q = q_ref[ts, lanes(h)]
                gs = (dot(ga, v_ref[:cols, lanes(h)], 1, 1) * decay_of(h, ts, cols)).astype(BF16)
                gq = gamma[ts] * dot(ga, frecv[h], 1, 1) + dot(gs, k_ref[:cols, lanes(h)], 1, 0)
                ki = dot(gs, q, 0, 0)
                vi = dot(sc_ref[h, ts, :cols], ga, 0, 0)
                q_ref[ts, lanes(h)] = gq.astype(BF16)
                for j in range(b + 1):
                    js = slice(j * tile, (j + 1) * tile)
                    kis[j] = ki[js] if kis[j] is None else kis[j] + ki[js]
                    vis[j] = vi[js] if vis[j] is None else vis[j] + vi[js]
            for j in range(tiles):
                js = slice(j * tile, (j + 1) * tile)
                k = k_ref[js, lanes(h)]
                gk = kis[j] + w[js] * dot(v_ref[js, lanes(h)], later, 1, 1)
                gv = vis[j] + w[js] * dot(k, later, 1, 0)
                k_ref[js, lanes(h)] = gk.astype(BF16)
                g_ref[js, lanes(h)] = gv.astype(BF16)

        each_head(g, one)
        pl.when(is_end)(lambda: ends_copy(g).start())
        gk_copy(g).start()

    def gk_copy(g):
        return pltpu.make_async_remote_copy(
            src_ref=k_ref.at[:, columns(g)], dst_ref=gm_ref.at[:, columns(g)],
            send_sem=gss.at[g], recv_sem=grs.at[g],
            device_id={"dp": mate}, device_id_type=MESH,
        )

    def ends_copy(g):
        return pltpu.make_async_remote_copy(
            src_ref=k_ref.at[:, columns(g)], dst_ref=ge_ref.at[pl.ds(0, B), columns(g)],
            send_sem=hss.at[g], recv_sem=hrs.at[g],
            device_id={"seq": hub}, device_id_type=MESH,
        )

    def pass_copy(g):
        return pltpu.make_async_remote_copy(
            src_ref=ge_ref.at[pl.ds(0, B), columns(g)], dst_ref=ge_ref.at[pl.ds(B, B), columns(g)],
            send_sem=mss.at[g], recv_sem=mrs.at[g],
            device_id={"dp": mate}, device_id_type=MESH,
        )

    def share(z, owner):
        return pl.ds(pl.multiple_of((z * 2 + owner) * rows, math.gcd(rows, LANES)), rows)

    def halves(which, base=0):
        return pl.ds(pl.multiple_of(base + which * half, math.gcd(half, LANES)), half)

    def x_copy(z):
        return pltpu.make_async_remote_copy(
            src_ref=xt_ref.at[share(z, mate)], dst_ref=xm_ref.at[z],
            send_sem=xss.at[z], recv_sem=xrs.at[z],
            device_id={"dp": mate}, device_id_type=MESH,
        )

    def turn(i, c):
        span = pl.ds(pl.multiple_of(i * LANES, LANES), LANES)
        xt_ref[span, :] = jnp.transpose(x_ref[:, span])
        return c

    def turn_inputs():
        load_x.wait()
        lax.fori_loop(0, D // LANES, turn, 0)

    def swap_inputs():
        lax.fori_loop(0, n, lambda e, c: (x_copy(far(e)).start(), c)[1], 0)

    def early_copy(e, part):
        z = far(e)
        src = (
            xt_ref.at[halves(side, (z * 2 + dp) * rows)] if part == 0 else xm_ref.at[z, halves(side)]
        )
        return pltpu.make_async_remote_copy(
            src_ref=src, dst_ref=xe_ref.at[z, halves(side), pl.ds(part * B, B)],
            send_sem=ess.at[z, part], recv_sem=ers.at[z, part],
            device_id={"seq": hub}, device_id_type=MESH,
        )

    def pair_copy(e, part, which):
        z = far(e)
        ref = xe_ref.at[z, halves(which), pl.ds(part * B, B)]
        return pltpu.make_async_remote_copy(
            src_ref=ref, dst_ref=ref, send_sem=pss.at[z, part], recv_sem=prs.at[z, part],
            device_id={"head": pair}, device_id_type=MESH,
        )

    def send_early(lo, hi):
        for j in range(lo, hi):
            if j % 2 == 1:
                x_copy(far(j // 2)).wait_recv()
            early_copy(j // 2, j % 2).start()

    def take_early(lo, hi):
        for j in range(lo, hi):
            early_copy(j // 2, j % 2).wait_recv()
            if paired:
                pair_copy(j // 2, j % 2, side).start()

    def have_early(lo, count):
        if paired:
            def one(e):
                for part in range(2):
                    pair_copy(lo + e, part, 1 - side).wait_recv()
            repeat(count, one)

    def partial(z, g):
        own = dot(xt_ref[share(z, dp), :], k_ref[:, columns(g)], 1, 0)
        return own + dot(xm_ref[z], gm_ref[:, columns(g)], 1, 0)

    def partial_extra(z, g):
        return partial(z, g) + dot(xe_ref[z], ge_ref[:, columns(g)], 1, 0)

    def term(z, g):
        down = (z < me).astype(jnp.int32)
        to = me + 1 - 2 * down
        slot = jnp.where((down == 1) & (to == z), n, z)
        return pltpu.make_async_remote_copy(
            src_ref=st_ref.at[z, g], dst_ref=st_ref.at[slot, g],
            send_sem=ss.at[z, g], recv_sem=rs.at[slot, g],
            device_id={"seq": to}, device_id_type=MESH,
        )

    def arrived(slot, g):
        pltpu.make_async_remote_copy(
            src_ref=st_ref.at[slot, g], dst_ref=st_ref.at[slot, g],
            send_sem=ss.at[0, g], recv_sem=rs.at[slot, g],
            device_id={"dp": mate}, device_id_type=MESH,
        ).wait_recv()

    def wait_x():
        @pl.when(inside)
        def _():
            lax.fori_loop(0, n, lambda z, c: (x_copy(z).wait_recv(), c)[1], 0)

        @pl.when(is_end)
        def _():
            x_copy(far(n - 1)).wait_recv()

    def take_factor(g):
        @pl.when(is_hub)
        def _():
            ends_copy(g).wait_recv()
            pass_copy(g).start()

    def send_share(e, g):
        z = far(e)
        pl.when(g == 0)(lambda: have_early(e, 1))
        st_ref[z, g] = partial_extra(z, g).astype(BF16)
        term(z, g).start()

    def send_first(g):
        gk_copy(g).wait_recv()

        @pl.when(is_hub)
        def _():
            pass_copy(g).wait_recv()
            send_share(0, g)

    def send_rest(g):
        pl.when(is_hub)(lambda: repeat(late - 1, lambda e: send_share(e + 1, g)))

    def pass_on(z, g):
        total = partial(z, g)
        arrived(z, g)
        st_ref[z, g] = (total + st_ref[z, g].astype(F32)).astype(BF16)
        term(z, g).start()

    def send_on(g):
        pl.when(is_hub)(lambda: pass_on(ext, g))
        if n > 4:
            @pl.when(jnp.logical_not(is_hub | is_end))
            def _():
                def step(j, c):
                    z = (j // 2) * (1 - j % 2) + (n - 1 - j // 2) * (j % 2)
                    pl.when(z != me)(lambda: pass_on(z, g))
                    return c
                lax.fori_loop(0, n, step, 0)

    def guarded(cond, body):
        pl.when(cond)(body)

    pieces = 2 * late
    most = pieces * 3 // 4
    pl.when(upper & inside)(turn_inputs)
    greeted()
    for a in range(2, 4):
        load(a, 2).start()
    pl.when(upper & inside)(swap_inputs)

    @pl.when(me == n - 1)
    def _():
        if 2 * rows % LANES == 0:
            spans = 2 * rows // LANES

            def share_turn(e):
                z = far(e)
                lax.fori_loop(z * spans, (z + 1) * spans, turn, 0)
                x_copy(z).start()

            load_x.wait()
            share_turn(0)
            send_early(0, 1)
            lax.fori_loop(1, n, lambda e, c: (share_turn(e), c)[1], 0)
        else:
            turn_inputs()
            swap_inputs()
            send_early(0, 1)
        send_early(1, most)

    ahead = min(groups, 4)

    def prepare(g):
        update(g)
        guarded(g >= ahead, lambda: relay_forward(g - ahead))

        @pl.when(inside & jnp.logical_not(upper) & (g == min(ahead, groups - 1)))
        def _():
            turn_inputs()
            swap_inputs()

    each_group(prepare)
    make_mask()

    @pl.when(me == 0)
    def _():
        turn_inputs()
        swap_inputs()
        send_early(0, pieces)

    behind = jnp.where(me == 0, groups - 1, jnp.minimum((n - 2 - me) * 2 + 1, groups - 1))
    products = groups + 1

    def iteration(i, c):
        done = i - groups
        guarded(i < ahead, lambda: relay_forward(i + groups - ahead))
        guarded(i < groups, lambda: attention(i))

        for q in range(3):
            lo, hi = pieces * q // 4, pieces * (q + 1) // 4
            at = max(0, groups - 4 + 2 * q)
            guarded(is_hub & (i == at), lambda: take_early(lo, hi))
        guarded((me == n - 1) & (i == 1), lambda: send_early(most, pieces))
        guarded(is_end & (done == 5), lambda: send_early(pieces, pieces + 2))
        guarded((done >= 0) & (done < groups), lambda: grads(done))
        guarded(is_hub & (done == 1), lambda: take_early(pieces * 3 // 4, pieces))

        guarded(i == products, wait_x)

        ready = i - products
        guarded((ready >= 1) & (ready <= groups // 2), lambda: send_rest(ready - 1))
        guarded((ready >= 0) & (ready < groups), lambda: take_factor(ready))
        guarded((ready >= 0) & (ready < groups), lambda: send_first(ready))
        guarded((ready > groups // 2) & (ready - 1 < groups), lambda: send_rest(ready - 1))
        guarded((ready >= 1) & (ready - 1 < groups), lambda: send_on(ready - 1))
        guarded(is_hub & (ready == 6), lambda: take_early(pieces, pieces + 2))
        guarded((i >= behind) & (i - behind < groups), lambda: relay_back(i - behind))
        return c

    lax.fori_loop(0, products + max(groups, 6) + 1, iteration, 0)

    def drain(g):
        @pl.when(me < n - 1)
        def _():
            forward(g).wait_send()

        @pl.when(me > 0)
        def _():
            backward(g).wait_send()

        gk_copy(g).wait_send()
        pl.when(is_end)(lambda: ends_copy(g).wait_send())
        pl.when(is_hub)(lambda: pass_copy(g).wait_send())

    each_group(drain)

    def sent_x(z, c):
        x_copy(z).wait_send()
        return c

    lax.fori_loop(0, n, sent_x, 0)

    def sent_early(e, c):
        for part in range(2):
            pl.when(is_end)(lambda: early_copy(e, part).wait_send())
            if paired:
                pl.when(is_hub)(lambda: pair_copy(e, part, side).wait_send())
        return c

    lax.fori_loop(0, n - 1, sent_early, 0)

    def settle(g):
        @pl.when(is_hub)
        def _():
            pl.when(g == 0)(lambda: have_early(late, 1))
            out_ref[:, columns(g)] = partial_extra(me, g)

        @pl.when(jnp.logical_not(is_hub))
        def _():
            out_ref[:, columns(g)] = partial(me, g)

        @pl.when(me > 1)
        def _():
            arrived(me, g)
            out_ref[:, columns(g)] += st_ref[me, g].astype(F32)

        @pl.when(me < n - 2)
        def _():
            arrived(n, g)
            out_ref[:, columns(g)] += st_ref[n, g].astype(F32)

        @pl.when(inside)
        def _():
            def step(z, c):
                pl.when(z != me)(lambda: term(z, g).wait_send())
                return c
            lax.fori_loop(0, n, step, 0)

    each_group(settle)


def layer(lengths, log_decay, x, q, k, v, g):
    heads, B = log_decay.shape
    D, F = x.shape[1], q.shape[1]
    n, group, groups, rows = sizes(heads, D)
    hbm = pl.BlockSpec(memory_space=pl.ANY)
    vmem = pl.BlockSpec(memory_space=pltpu.VMEM)
    state = (heads, LANES, LANES)
    wide = pltpu.VMEM((B, F), BF16)
    dma = pltpu.SemaphoreType.DMA
    return pl.pallas_call(
        functools.partial(layer_kernel, heads),
        out_shape=(wide, wide, pltpu.VMEM((rows, F), F32)),
        in_specs=[
            pl.BlockSpec(memory_space=pltpu.SMEM), pl.BlockSpec(memory_space=pltpu.VMEM)
        ] + [hbm] * 5,
        out_specs=(vmem, vmem, vmem),
        scratch_shapes=[pltpu.VMEM((B, F), BF16)] * 2
        + [
            pltpu.VMEM((B, D), BF16),
            pltpu.VMEM((D, B), BF16),
            pltpu.VMEM((n, rows, B), BF16),
            pltpu.VMEM((n, rows, 2 * B), BF16),
            pltpu.VMEM((B, F), BF16),
            pltpu.VMEM((2 * B, F), BF16),
            pltpu.VMEM((n + 1, groups, rows, group * LANES), BF16),
            pltpu.VMEM((heads, B), F32),
            pltpu.VMEM((heads, B, LANES), F32),
            pltpu.VMEM((B, B), F32),
            pltpu.VMEM((B, LANES), F32),
            pltpu.VMEM((B, LANES), F32),
            pltpu.VMEM(state, F32),
            pltpu.VMEM((heads, B, B), BF16),
            pltpu.VMEM((heads, B, LANES), BF16),
            pltpu.VMEM(state, F32),
        ]
        + [pltpu.VMEM(state, BF16)] * 4
        + [dma((groups,))] * 4
        + [
            dma((4, 2)), dma(()), dma((n,)), dma((n,)),
            dma((groups,)), dma((groups,)), dma((n, groups)), dma((n + 1, groups)),
        ]
        + [dma((n, 2))] * 4 + [dma((groups,))] * 4,
        compiler_params=pltpu.CompilerParams(
            collective_id=0, has_side_effects=True, vmem_limit_bytes=55 * 1024 * 1024
        ),
        name="layer",
    )(lengths, log_decay, x, q, k, v, g)


def deliver_kernel(*refs):
    count = (len(refs) - 1) // 2
    srcs, dsts, sem = refs[:count], refs[count:-1], refs[-1]
    moves = [pltpu.make_async_copy(srcs[a], dsts[a], sem.at[a]) for a in range(count)]
    for move in moves:
        move.start()
    for move in moves:
        move.wait()


def deliver(*arrays):
    hbm = pl.BlockSpec(memory_space=pl.ANY)
    vmem = pl.BlockSpec(memory_space=pltpu.VMEM)
    return pl.pallas_call(
        deliver_kernel,
        out_shape=tuple(jax.ShapeDtypeStruct(a.shape, a.dtype) for a in arrays),
        in_specs=[vmem] * len(arrays),
        out_specs=(hbm,) * len(arrays),
        scratch_shapes=[pltpu.SemaphoreType.DMA((len(arrays),))],
        compiler_params=pltpu.CompilerParams(vmem_limit_bytes=16 * 1024 * 1024),
        name="deliver",
    )(*arrays)


def body(inputs, queries, keys, values, log_decay, list_lengths, grad_out):
    gq, gv, gw = layer(
        list_lengths, log_decay[0], inputs[0], queries[0], keys[0], values[0], grad_out[0]
    )
    gq, gv, gw = deliver(gq, gv, gw)
    return gq[None], gv[None], gw


def solution(mesh):
    rows = ("groups", "dp")
    wide = P(rows, "seq", "head")
    return jax.shard_map(
        body,
        mesh=mesh,
        in_specs=(
            P(rows, "seq", None), wide, wide, wide, P(rows, "head", "seq"), P(rows, None), wide,
        ),
        out_specs=(wide, wide, P(("groups", "seq", "dp"), "head")),
        check_vma=False,
    )
```
